32 devices in a mesh: grp: 2 (over x), seq: 8 (over z, y), head: 2 (over core).
Axes of the slice: x: 2, y: 2, z: 4, core: 2. Of those that a mesh axis runs over, the one named last changes fastest.
Arguments:
- x_in: bfloat16 [8192, 4096], P(('grp', 'seq'), 'head'), parts along dimension 0, may hold values from -6 to 6
- z_gate: bfloat16 [8192, 4096], P(('grp', 'seq'), 'head'), parts along dimension 0, may hold values from -6 to 6
- b_proj: bfloat16 [8192, 128], P(('grp', 'seq')), parts along dimension 0, may hold values from -2 to 2
- c_proj: bfloat16 [8192, 128], P(('grp', 'seq')), parts along dimension 0, may hold values from -2 to 2
- step_size: float32 [8192, 64], P(('grp', 'seq'), 'head'), parts along dimension 0, may hold values from 0 to 2, as said below
- log_decay: float32 [8192, 64], P(('grp', 'seq'), 'head'), parts along dimension 0, may hold values from -1 to 0, as said below
- conv_weight: float32 [4, 4096], P(None, 'head'), may hold values from -3 to 3
- skip_gain: float32 [64], P('head'), may hold values from 0.5 to 2
- norm_gain: float32 [4096], P('head'), may hold values from 0.5 to 1.5
Outputs:
- mixed: bfloat16 [8192, 4096], P(('grp', 'seq'), 'head'), parts along dimension 0
The draws below stay inside these ranges and needn't reach their ends.
There are 2 independent parts, one for each index of `grp`. The reference program is written for one: setup_inputs(seed, part) draws one part's arguments, and reference() takes and returns one part's arrays. A program takes and returns all parts, laid end to end along the dimension named above; an argument that names none is the same for every part. Nothing has to cross between parts.
Inputs may be any that keep to these rules, and one draw needn't show every extreme that they name: `step_size`: step sizes are positive. `log_decay`: every entry is negative.
All inputs are finite; a program needn't handle non-finite values.
Results may differ from the reference program's by a relative error of at most 0.0057.
Values may be sent and summed in bfloat16 or wider, within the bound.
A program may use at most 192 MiB of HBM per device.

```python
import math
import jax
import jax.numpy as jnp
from jax import lax

HEAD_COUNT = 64
HEAD_DIM = 64
STATE = 128
SPAN = 256
KCONV = 4
TOK_DEV = 512
WIDTH = 4096
TOKEN_POSITIONS = 4096


def decay_and_steps(key):
    random_keys = jax.random.split(jax.random.fold_in(key, 7), 7)
    share_fast = 0.5
    fast_heads = jax.random.bernoulli(random_keys[0], share_fast, (HEAD_COUNT,))
    fast_rate = jax.random.uniform(random_keys[1], (HEAD_COUNT,), jnp.float32, 1.0 / 50.0, 1.0 / 30.0)
    slow_rate = 0.25 * 2.302585 / TOKEN_POSITIONS
    decay_rate = jnp.where(fast_heads, fast_rate, slow_rate)
    spread = jnp.log(2.0)
    position_multiplier = jnp.exp(jax.random.uniform(random_keys[2], (TOKEN_POSITIONS, HEAD_COUNT), jnp.float32, -spread, spread))
    block_draw = jnp.exp(jax.random.uniform(random_keys[3], (TOKEN_POSITIONS // TOK_DEV, HEAD_COUNT), jnp.float32, -spread, spread))
    block_multiplier = jnp.repeat(block_draw, TOK_DEV, axis=0)
    jump_position = jax.random.randint(random_keys[4], (3,), 0, TOKEN_POSITIONS)
    match_count = jnp.any(jnp.arange(TOKEN_POSITIONS)[:, None] == jump_position[None, :], axis=1)
    sudden_jump = jax.random.uniform(random_keys[5], (TOKEN_POSITIONS, HEAD_COUNT), jnp.float32, 0.22, 0.7)
    logarithm_values = -(decay_rate[None, :] * position_multiplier * block_multiplier) - jnp.where(match_count[:, None], sudden_jump, 0.0)
    step_base = jnp.exp(jax.random.uniform(random_keys[6], (TOKEN_POSITIONS, HEAD_COUNT), jnp.float32, -spread, spread))
    steps = step_base * jnp.sqrt(jnp.minimum(1.0, 40.0 * decay_rate))[None, :]
    return (logarithm_values, steps)


def draw_step_size(key, part):
    return decay_and_steps(key)[1]


def draw_log_decay(key, part):
    return decay_and_steps(key)[0]


def level_of(own_key, extent, cuts, least, top_value):
    def one(axis_at, parts):
        steps = jax.random.uniform(jax.random.fold_in(jax.random.fold_in(own_key, 6), axis_at), (parts,), jnp.float32, least / len(cuts), top_value / len(cuts))
        return jnp.repeat(jnp.exp(steps), extent[axis_at] // parts).reshape((-1,) + (1,) * (len(extent) - axis_at - 1))

    level = one(*cuts[0])
    for cut in cuts[1:]:
        level = level * one(*cut)
    return level


def normal_values(stream_key, shape, width, most, cuts=(), held_as=jnp.bfloat16):
    array = jax.random.normal(stream_key, shape, jnp.float32) * width
    if len(cuts) > 0:
        array = level_of(stream_key, shape, cuts, -0.22, 0.18) * array
    return jnp.clip(array, min=-most, max=most).astype(held_as)


def setup_inputs(seed: int = 0, part: int = 0) -> dict:
    streams_of = jax.random.split(jax.random.key(seed), 10)
    own_keys = jax.random.split(jax.random.fold_in(streams_of[9], part), 10)
    return {
        "x_in": normal_values(own_keys[0], (TOKEN_POSITIONS, WIDTH), 1.0, 6.0, ((0, 8), (1, 2))),
        "z_gate": normal_values(own_keys[1], (TOKEN_POSITIONS, WIDTH), 1.0, 6.0, ((0, 8), (1, 2))),
        "b_proj": normal_values(own_keys[2], (TOKEN_POSITIONS, STATE), 0.3, 2.0, ((0, 8),)),
        "c_proj": normal_values(own_keys[3], (TOKEN_POSITIONS, STATE), 0.3, 2.0, ((0, 8),)),
        "step_size": draw_step_size(jax.random.fold_in(jax.random.fold_in(streams_of[9], part), 71), part),
        "log_decay": draw_log_decay(jax.random.fold_in(jax.random.fold_in(streams_of[9], part), 71), part),
        "conv_weight": normal_values(streams_of[6], (KCONV, WIDTH), KCONV ** -0.5, 3.0, ((1, 2),), jnp.float32),
        "skip_gain": jnp.clip(jnp.exp(math.log(2.0) - 1.3862944 * jax.random.uniform(streams_of[7], (HEAD_COUNT,), jnp.float32) ** level_of(streams_of[7], (HEAD_COUNT,), ((0, 2),), -0.2, 0.2)), 0.5, 2.0),
        "norm_gain": jnp.clip(1.0 + 0.1 * jax.random.normal(streams_of[8], (WIDTH,), jnp.float32), 0.5, 1.5),
    }


def conv_pair(x_in, conv_weight):
    length = x_in.shape[0]
    reach = KCONV - 1
    padded = jnp.pad(x_in.astype(jnp.float32), ((reach, reach), (0, 0)))
    forward = jnp.zeros((length, x_in.shape[1]), jnp.float32)
    backward = jnp.zeros((length, x_in.shape[1]), jnp.float32)
    for tap in range(KCONV):
        forward = forward + conv_weight[tap] * padded[tap:tap + length]
        backward = backward + conv_weight[tap] * padded[2 * reach - tap:2 * reach - tap + length]
    return (jax.nn.silu(forward).astype(jnp.bfloat16), jax.nn.silu(backward).astype(jnp.bfloat16))

def span_step(state, pieces):
    x_block, b_block, c_block, step_block, decay_block = pieces
    cumul = jnp.cumsum(decay_block, axis=0)
    gram_mat = jnp.dot(c_block, b_block.T, preferred_element_type=jnp.float32)
    segment = cumul.T[:, :, None] - cumul.T[:, None, :]
    row_ids = jnp.arange(SPAN)
    lower_mask = row_ids[:, None] >= row_ids[None, :]
    decay_mat = jnp.exp(jnp.where(lower_mask[None], segment, -1e+30))
    weights = (gram_mat[None] * decay_mat * step_block.T[:, None, :]).astype(jnp.bfloat16)
    result = jnp.einsum('hts,shp->thp', weights.astype(jnp.float32), x_block.astype(jnp.float32))
    carried = c_block.astype(jnp.float32)[:, None, :] * jnp.exp(cumul)[:, :, None]
    result = result + jnp.einsum('thn,hnp->thp', carried, state, precision=lax.Precision.HIGHEST)
    to_end = jnp.exp(cumul[-1][None, :] - cumul) * step_block
    b_weighted = (b_block.astype(jnp.float32)[:, None, :] * to_end[:, :, None]).astype(jnp.bfloat16)
    contrib = jnp.einsum('shn,shp->hnp', b_weighted.astype(jnp.float32), x_block.astype(jnp.float32))
    state = jnp.exp(cumul[-1])[:, None, None] * state + contrib
    return (state, result)

def strand_scan(x_three, b_proj, c_proj, step_size, log_decay):
    count = TOKEN_POSITIONS // SPAN
    pieces = (x_three.reshape(count, SPAN, HEAD_COUNT, HEAD_DIM), b_proj.reshape(count, SPAN, STATE), c_proj.reshape(count, SPAN, STATE), step_size.reshape(count, SPAN, HEAD_COUNT), log_decay.reshape(count, SPAN, HEAD_COUNT))
    start = jnp.zeros((HEAD_COUNT, STATE, HEAD_DIM), jnp.float32)
    final, outputs = lax.scan(span_step, start, pieces)
    return outputs.reshape(TOKEN_POSITIONS, HEAD_COUNT, HEAD_DIM)

def reference(x_in, z_gate, b_proj, c_proj, step_size, log_decay, conv_weight, skip_gain, norm_gain):
    conv_fwd, conv_rev = conv_pair(x_in, conv_weight)
    three_fwd = conv_fwd.reshape(TOKEN_POSITIONS, HEAD_COUNT, HEAD_DIM)
    three_rev = conv_rev.reshape(TOKEN_POSITIONS, HEAD_COUNT, HEAD_DIM)
    y_fwd = strand_scan(three_fwd, b_proj, c_proj, step_size, log_decay)
    y_rev = jnp.flip(strand_scan(jnp.flip(three_rev, 0), jnp.flip(b_proj, 0), jnp.flip(c_proj, 0), jnp.flip(step_size, 0), jnp.flip(log_decay, 0)), 0)
    total = y_fwd + y_rev + skip_gain[None, :, None] * (three_fwd.astype(jnp.float32) + three_rev.astype(jnp.float32))
    gated = total.reshape(TOKEN_POSITIONS, WIDTH) * jax.nn.silu(z_gate.astype(jnp.float32))
    meansq = lax.optimization_barrier(jnp.mean(gated * gated, axis=1, keepdims=True))
    return (gated * lax.rsqrt(meansq + 1e-05) * norm_gain).astype(jnp.bfloat16)
```

```python
import functools

import jax
import jax.numpy as jnp
from jax import lax
from jax.experimental import pallas as pl
from jax.experimental.pallas import tpu as pltpu
from jax.sharding import PartitionSpec as P

SPAN = 256
KCONV = 4
EPS = 1e-05
TILE = 256
MESH = pl.DeviceIdType.MESH
F32 = jnp.float32
BF16 = jnp.bfloat16
HIGH = lax.Precision.HIGHEST


def mm(a, b):
    return jnp.dot(a, b, preferred_element_type=F32)


def split_three(a):
    hi = a.astype(BF16)
    rest = a - hi.astype(F32)
    mid = rest.astype(BF16)
    low = (rest - mid.astype(F32)).astype(BF16)
    return hi, mid, low


def silu(v):
    return v * pl.reciprocal(1.0 + jnp.exp(-v))


def prelude_kernel(ld_ref, step_ref, b_ref, c_ref, quant_ref, col_ref, row_ref, gram_ref, held):
    tok, heads = ld_ref.shape
    per_tile = col_ref.shape[2] // 2
    rows = lax.broadcasted_iota(jnp.int32, (SPAN, SPAN), 0)
    cols = lax.broadcasted_iota(jnp.int32, (SPAN, SPAN), 1)
    tri = jnp.where(rows >= cols, 1.0, 0.0).astype(BF16)
    for j in range(tok // SPAN):
        here = pl.ds(j * SPAN, SPAN)
        decay = ld_ref[here, :]
        step = step_ref[here, :]
        hi, mid, low = split_three(decay)
        cs = mm(tri, hi) + mm(tri, mid) + mm(tri, low)
        ecs = cs - decay
        last = cs[SPAN - 1 : SPAN, :]
        held[here, 0:heads] = jnp.exp(last - cs) * step
        held[here, heads : 2 * heads] = jnp.exp(ecs) * step
        held[here, 2 * heads : 3 * heads] = jnp.exp(cs)
        held[here, 3 * heads : 4 * heads] = jnp.exp(last - ecs)
        log_step = jnp.log(step)
        row_ref[0, :, here] = (cs - log_step).T
        row_ref[1, :, here] = (ecs + log_step).T
        for g in range(heads // per_tile):
            part = slice(g * per_tile, (g + 1) * per_tile)
            col_ref[g, here, 0:per_tile] = cs[:, part]
            col_ref[g, here, per_tile : 2 * per_tile] = ecs[:, part]
        gram_ref[j] = lax.dot_general(
            c_ref[here, :], b_ref[here, :], (((1,), (1,)), ((), ())), preferred_element_type=F32
        )
    full = held[...]
    hi = full.astype(BF16)
    quant_ref[:, 0 : 4 * heads] = hi
    quant_ref[:, 4 * heads : 8 * heads] = (full - hi.astype(F32)).astype(BF16)


def selector(tile, which, heads, head_dim):
    shape = (8 * heads, TILE)
    row = lax.broadcasted_iota(jnp.int32, shape, 0)
    lane = lax.broadcasted_iota(jnp.int32, shape, 1)
    want = which * heads + tile * (TILE // head_dim) + lane // head_dim
    return jnp.where((row == want) | (row == want + 4 * heads), 1.0, 0.0).astype(BF16)


def conv_kernel(heads, x_ref, low_ref, high_ref, w_ref, bt_ref, quant_ref, fwd_ref, rev_ref,
                end_f_ref, end_r_ref, loc_f_ref, loc_r_ref, pad):
    tok = x_ref.shape[0]
    head_dim = pl.num_programs(0) * TILE // heads
    tile = pl.program_id(0)
    reach = KCONV - 1
    pad[pl.ds(8, tok), :] = x_ref[...].astype(F32)
    pad[pl.ds(8 - reach, reach), :] = low_ref[...].astype(F32)
    pad[pl.ds(8 + tok, reach), :] = high_ref[...].astype(F32)
    sel = [selector(tile, q, heads, head_dim) for q in range(4)]
    ends = []
    for j in range(tok // SPAN):
        first = j * SPAN
        fwd = jnp.zeros((SPAN, TILE), F32)
        rev = jnp.zeros((SPAN, TILE), F32)
        for k in range(KCONV):
            w = w_ref[k : k + 1, :]
            fwd = fwd + w * pad[pl.ds(8 - reach + k + first, SPAN), :]
            rev = rev + w * pad[pl.ds(8 + reach - k + first, SPAN), :]
        here = pl.ds(first, SPAN)
        fwd = silu(fwd).astype(BF16)
        rev = silu(rev).astype(BF16)
        fwd_ref[here, :] = fwd
        rev_ref[here, :] = rev
        quant = quant_ref[here, :]
        to_f = (fwd.astype(F32) * mm(quant, sel[0])).astype(BF16)
        to_r = (rev.astype(F32) * mm(quant, sel[1])).astype(BF16)
        bt = bt_ref[:, here]
        ends.append((mm(bt, to_f), mm(bt, to_r)))
    last = mm(quant_ref[pl.ds(tok - 8, 8), :], sel[2])[7:8, :]
    first = mm(quant_ref[pl.ds(0, 8), :], sel[3])[0:1, :]
    (f0, r0), (f1, r1) = ends
    end_f_ref[0] = (last * f0 + f1).astype(BF16)
    end_r_ref[0] = (first * r1 + r0).astype(BF16)
    loc_f_ref[0] = f0.astype(BF16)
    loc_r_ref[0] = r1.astype(BF16)


def carry_kernel(count, heads, f_ref, r_ref, tot_ref, in_f_ref, in_r_ref, coef, out_chain,
                 out_swap, got_chain, got_swap, send_chain, send_swap, recv_chain, recv_swap):
    tiles = f_ref.shape[0]
    place = lax.axis_index("seq")
    lines = count // 2
    line = place // 2
    side = place - 2 * line
    partner = place + 1 - 2 * side

    barrier = pltpu.get_barrier_semaphore()
    pl.semaphore_signal(barrier, inc=1, device_id={"seq": partner}, device_id_type=MESH)

    @pl.when(line > 0)
    def _():
        pl.semaphore_signal(barrier, inc=1, device_id={"seq": place - 2}, device_id_type=MESH)

    @pl.when(line < lines - 1)
    def _():
        pl.semaphore_signal(barrier, inc=1, device_id={"seq": place + 2}, device_id_type=MESH)

    width = tiles * TILE
    head = lax.broadcasted_iota(jnp.int32, (heads, width), 0)
    lane = lax.broadcasted_iota(jnp.int32, (heads, width), 1)
    spread = jnp.where(lane // (width // heads) == head, 1.0, 0.0).astype(BF16)
    hi, mid, low = split_three(jnp.exp(tot_ref[...]))
    wide = mm(hi, spread) + mm(mid, spread) + mm(low, spread)
    for i in range(tiles):
        coef[i] = wide[:, i * TILE : (i + 1) * TILE]

    pl.semaphore_wait(
        barrier, 1 + jnp.where(line > 0, 1, 0) + jnp.where(line < lines - 1, 1, 0)
    )

    def chain_copy(strand, i, to):
        return pltpu.make_async_remote_copy(
            src_ref=out_chain.at[strand, i],
            dst_ref=got_chain.at[strand, i],
            send_sem=send_chain.at[strand, i],
            recv_sem=recv_chain.at[strand, i],
            device_id={"seq": to},
            device_id_type=MESH,
        )

    def swap_copy(strand, i):
        return pltpu.make_async_remote_copy(
            src_ref=out_swap.at[strand, i],
            dst_ref=got_swap.at[strand, i],
            send_sem=send_swap.at[strand, i],
            recv_sem=recv_swap.at[strand, i],
            device_id={"seq": partner},
            device_id_type=MESH,
        )

    strands = (
        (0, f_ref, in_f_ref, line, side, place + 2, place - 2),
        (1, r_ref, in_r_ref, lines - 1 - line, 1 - side, place - 2, place + 2),
    )

    def turn(s, _):
        for strand, end_ref, in_ref, depth, second, after, before in strands:
            i = s - depth

            @pl.when((i >= 0) & (i < tiles))
            def _():
                early = jnp.where(second == 0, 1.0, 0.0)
                own = coef[i][0:1, :]
                other = coef[i][1:2, :]
                end = end_ref[i].astype(F32)

                @pl.when(depth > 0)
                def _():
                    chain_copy(strand, i, before).wait_recv()

                @pl.when(depth == 0)
                def _():
                    got_chain[strand, i] = jnp.zeros(got_chain.shape[2:], BF16)

                came = got_chain[strand, i].astype(F32)
                with_own = early * (own * came + end) + (1.0 - early) * came
                out_swap[strand, i] = with_own.astype(BF16)
                swap_copy(strand, i).start()

                @pl.when(depth < lines - 1)
                def _():
                    grown = early * other + (1.0 - early)
                    out_chain[strand, i] = (own * other * came + grown * end).astype(BF16)
                    chain_copy(strand, i, after).start()

        return 0

    lax.fori_loop(0, tiles + lines - 1, turn, 0)

    def finish(i, _):
        for strand, end_ref, in_ref, depth, second, after, before in strands:
            early = jnp.where(second == 0, 1.0, 0.0)
            other = coef[i][1:2, :]
            swap_copy(strand, i).wait()
            came = got_chain[strand, i].astype(F32)
            kept = (early + (1.0 - early) * other) * came
            in_ref[i] = (kept + got_swap[strand, i].astype(F32)).astype(BF16)

            @pl.when(depth < lines - 1)
            def _():
                chain_copy(strand, i, after).wait_send()

        return 0

    lax.fori_loop(0, tiles, finish, 0)


def mix_kernel(heads, fwd_ref, rev_ref, z_ref, c_ref, quant_ref, col_ref, row_ref, gram_ref,
               in_f_ref, in_r_ref, loc_f_ref, loc_r_ref, skip_ref, gated_ref, sum_ref, acc):
    tok = fwd_ref.shape[0]
    head_dim = pl.num_programs(0) * TILE // heads
    per_tile = TILE // head_dim
    pair = 128 // head_dim
    tile = pl.program_id(0)
    rows = lax.broadcasted_iota(jnp.int32, (SPAN, SPAN), 0)
    cols = lax.broadcasted_iota(jnp.int32, (SPAN, SPAN), 1)
    lower = rows >= cols
    upper = rows <= cols
    lane = lax.broadcasted_iota(jnp.int32, (SPAN, 128), 1) // head_dim
    sel_f = selector(tile, 2, heads, head_dim)
    sel_r = selector(tile, 3, heads, head_dim)

    @pl.when(tile == 0)
    def _():
        acc[...] = jnp.zeros_like(acc)

    in_f = in_f_ref[0]
    in_r = in_r_ref[0]
    wide_f = [mm(quant_ref[pl.ds(j * SPAN, SPAN), :], sel_f) for j in range(2)]
    wide_r = [mm(quant_ref[pl.ds(j * SPAN, SPAN), :], sel_r) for j in range(2)]
    next_f = loc_f_ref[0].astype(F32) + wide_f[0][SPAN - 1 : SPAN, :] * in_f.astype(F32)
    next_r = loc_r_ref[0].astype(F32) + wide_r[1][0:1, :] * in_r.astype(F32)
    start_f = (in_f, next_f.astype(BF16))
    start_r = (next_r.astype(BF16), in_r)
    for j in range(2):
        here = pl.ds(j * SPAN, SPAN)
        gram = gram_ref[j]
        c_rows = c_ref[here, :]
        carried = wide_f[j] * mm(c_rows, start_f[j]) + wide_r[j] * mm(c_rows, start_r[j])
        for p in range(TILE // 128):
            lanes = slice(p * 128, (p + 1) * 128)
            fwd = fwd_ref[here, lanes]
            rev = rev_ref[here, lanes]
            total = None
            for q in range(pair):
                h = p * pair + q
                cs = col_ref[0, here, h : h + 1]
                ecs = col_ref[0, here, per_tile + h : per_tile + h + 1]
                row_a = row_ref[0, 0, h : h + 1, here]
                row_b = row_ref[1, 0, h : h + 1, here]
                weights = gram * jnp.exp(jnp.where(lower, cs - row_a, row_b - ecs))
                low = jnp.where(lower, weights, 0.0).astype(BF16)
                up = jnp.where(upper, weights, 0.0).astype(BF16)
                got = mm(low, fwd) + mm(up, rev)
                total = got if total is None else jnp.where(lane >= q, got, total)
            total = total + carried[:, lanes]
            total = total + skip_ref[0:1, lanes] * (fwd.astype(F32) + rev.astype(F32))
            gated = total * silu(z_ref[here, lanes].astype(F32))
            gated_ref[here, lanes] = gated.astype(BF16)
            acc[here, :] += gated * gated

    @pl.when(tile == pl.num_programs(0) - 1)
    def _():
        sum_ref[...] = lax.dot_general(
            jnp.ones((8, 128), F32), acc[...], (((1,), (1,)), ((), ())),
            preferred_element_type=F32, precision=HIGH,
        )


def scale_kernel(width, gated_ref, sum_ref, other_ref, gain_ref, out_ref):
    total = sum_ref[...] + other_ref[...]
    pick = jnp.where(lax.broadcasted_iota(jnp.int32, (8, 128), 0) == 0, 1.0, 0.0)
    square = lax.dot_general(
        total, pick, (((0,), (0,)), ((), ())), preferred_element_type=F32, precision=HIGH
    )
    scale = lax.rsqrt(square / width + EPS)
    for p in range(out_ref.shape[1] // 128):
        lanes = slice(p * 128, (p + 1) * 128)
        out_ref[:, lanes] = (
            gated_ref[:, lanes].astype(F32) * scale * gain_ref[0:1, lanes]
        ).astype(BF16)


def on_device(count, head_count, x_in, z_gate, b_proj, c_proj, step_size, log_decay, conv_weight,
              skip_gain, norm_gain):
    tok, chan = x_in.shape
    heads = step_size.shape[1]
    head_dim = chan // heads
    state = b_proj.shape[1]
    tiles = chan // TILE
    per_tile = TILE // head_dim
    reach = KCONV - 1
    blocks = tok // SPAN
    up = [(i, i + 1) for i in range(count - 1)]
    down = [(i + 1, i) for i in range(count - 1)]
    swap = [(i, i + 1 - 2 * (i % 2)) for i in range(count)]
    low = lax.ppermute(x_in[tok - reach :], "seq", up)
    high = lax.ppermute(x_in[:reach], "seq", down)
    own_total = jnp.sum(log_decay, axis=0, keepdims=True)
    totals = jnp.concatenate(
        [own_total, lax.ppermute(own_total, "seq", swap), jnp.zeros((6, heads), F32)], axis=0
    )

    sds = jax.ShapeDtypeStruct
    whole = pl.BlockSpec(memory_space=pltpu.VMEM)
    quant, col, row, gram = pl.pallas_call(
        prelude_kernel,
        out_shape=(
            sds((tok, 8 * heads), BF16),
            sds((tiles, tok, 2 * per_tile), F32),
            sds((2, heads, tok), F32),
            sds((blocks, SPAN, SPAN), F32),
        ),
        in_specs=[whole] * 4,
        out_specs=[whole] * 4,
        scratch_shapes=[pltpu.VMEM((tok, 4 * heads), F32)],
        cost_estimate=pl.CostEstimate(
            flops=200_000_000, bytes_accessed=4_000_000, transcendentals=100_000
        ),
        name="prelude",
    )(log_decay, step_size, b_proj, c_proj)
    row = row.reshape(2, tiles, per_tile, tok)

    def full(*shape):
        return pl.BlockSpec(shape, lambda i: (0,) * len(shape))

    tall = pl.BlockSpec((tok, TILE), lambda i: (0, i))
    halo = pl.BlockSpec((reach, TILE), lambda i: (0, i))
    chunk = pl.BlockSpec((1, state, TILE), lambda i: (i, 0, 0))
    states = sds((tiles, state, TILE), BF16)
    big = pltpu.CompilerParams(vmem_limit_bytes=56 << 20)
    fwd, rev, end_f, end_r, loc_f, loc_r = pl.pallas_call(
        functools.partial(conv_kernel, heads),
        grid=(tiles,),
        out_shape=(sds((tok, chan), BF16), sds((tok, chan), BF16), states, states, states, states),
        in_specs=[tall, halo, halo, pl.BlockSpec((KCONV, TILE), lambda i: (0, i)),
                  full(state, tok), full(tok, 8 * heads)],
        out_specs=[tall, tall, chunk, chunk, chunk, chunk],
        scratch_shapes=[pltpu.VMEM((tok + 16, TILE), F32)],
        compiler_params=big,
        name="conv",
    )(x_in, low, high, conv_weight, b_proj.T, quant)

    slots = pltpu.VMEM((2, tiles, state, TILE), BF16)
    sems = pltpu.SemaphoreType.DMA((2, tiles))
    in_f, in_r = pl.pallas_call(
        functools.partial(carry_kernel, count, heads),
        out_shape=(states, states),
        in_specs=[whole] * 3,
        out_specs=[whole] * 2,
        scratch_shapes=[pltpu.VMEM((tiles, 8, TILE), F32), slots, slots, slots, slots,
                        sems, sems, sems, sems],
        compiler_params=pltpu.CompilerParams(collective_id=0, has_side_effects=True),
        name="carry",
    )(end_f, end_r, totals)

    gated, sums = pl.pallas_call(
        functools.partial(mix_kernel, heads),
        grid=(tiles,),
        out_shape=(sds((tok, chan), BF16), sds((8, tok), F32)),
        in_specs=[tall, tall, tall, full(tok, state), full(tok, 8 * heads),
                  pl.BlockSpec((1, tok, 2 * per_tile), lambda i: (i, 0, 0)),
                  pl.BlockSpec((2, 1, per_tile, tok), lambda i: (0, i, 0, 0)),
                  full(blocks, SPAN, SPAN), chunk, chunk, chunk, chunk,
                  pl.BlockSpec((1, TILE), lambda i: (0, i))],
        out_specs=[tall, full(8, tok)],
        scratch_shapes=[pltpu.VMEM((tok, 128), F32)],
        compiler_params=big,
        name="mix",
    )(fwd, rev, z_gate, c_proj, quant, col, row, gram, in_f, in_r, loc_f, loc_r,
      jnp.repeat(skip_gain, head_dim)[None, :])

    others = jnp.zeros_like(sums)
    for turn in range(1, head_count):
        others = others + lax.ppermute(
            sums, "head", [(i, (i + turn) % head_count) for i in range(head_count)]
        )
    return pl.pallas_call(
        functools.partial(scale_kernel, head_count * chan),
        grid=(2,),
        out_shape=sds((tok, chan), BF16),
        in_specs=[pl.BlockSpec((tok, chan // 2), lambda i: (0, i)), full(8, tok), full(8, tok),
                  pl.BlockSpec((1, chan // 2), lambda i: (0, i))],
        out_specs=pl.BlockSpec((tok, chan // 2), lambda i: (0, i)),
        compiler_params=big,
        name="scale",
    )(gated, sums, others, norm_gain[None, :])


def solution(mesh):
    return jax.shard_map(
        functools.partial(on_device, mesh.shape["seq"], mesh.shape["head"]),
        mesh=mesh,
        in_specs=(
            P(("grp", "seq"), "head"),
            P(("grp", "seq"), "head"),
            P(("grp", "seq"), None),
            P(("grp", "seq"), None),
            P(("grp", "seq"), "head"),
            P(("grp", "seq"), "head"),
            P(None, "head"),
            P("head"),
            P("head"),
        ),
        out_specs=P(("grp", "seq"), "head"),
        check_vma=False,
    )
```

```python
import functools

import jax
import jax.numpy as jnp
from jax import lax
from jax.experimental import pallas as pl
from jax.experimental.pallas import tpu as pltpu
from jax.sharding import PartitionSpec as P

SPAN = 256
KCONV = 4
EPS = 1e-05
TILE = 256
MESH = pl.DeviceIdType.MESH
F32 = jnp.float32
BF16 = jnp.bfloat16
HIGH = lax.Precision.HIGHEST


def mm(a, b):
    return jnp.dot(a, b, preferred_element_type=F32)


def split_three(a):
    hi = a.astype(BF16)
    rest = a - hi.astype(F32)
    mid = rest.astype(BF16)
    low = (rest - mid.astype(F32)).astype(BF16)
    return hi, mid, low


def silu(v):
    return v * pl.reciprocal(1.0 + jnp.exp(-v))


def selector(tile, which, heads, head_dim):
    shape = (8 * heads, TILE)
    row = lax.broadcasted_iota(jnp.int32, shape, 0)
    lane = lax.broadcasted_iota(jnp.int32, shape, 1)
    want = which * heads + tile * (TILE // head_dim) + lane // head_dim
    return jnp.where((row == want) | (row == want + 4 * heads), 1.0, 0.0).astype(BF16)


LAG = 2


def mixer_kernel(count, head_count, x_ref, z_ref, b_ref, c_ref, step_ref, ld_ref, w_ref, skip_ref,
                 gain_ref, out_ref, low, high, tot, wide, held, quant, cols, rows_ab, gram, pad,
                 fwd_all, rev_all, total_all, end_all, loc_f, loc_r, out_chain, out_swap,
                 got_chain, got_swap, acc, sums, sums_got, send_chain, send_swap, recv_chain,
                 recv_swap, send_small, recv_small, send_sum, recv_sum):
    tok, chan = x_ref.shape
    heads = step_ref.shape[0]
    head_dim = chan // heads
    state = b_ref.shape[1]
    tiles = chan // TILE
    per_tile = TILE // head_dim
    pair = 128 // head_dim
    blocks = tok // SPAN
    reach = KCONV - 1
    edge = low.shape[0]
    place = lax.axis_index("seq")
    lines = count // 2
    line = place // 2
    side = place - 2 * line
    partner = place + 1 - 2 * side
    me = lax.axis_index("head")

    barrier = pltpu.get_barrier_semaphore()
    ready = head_count - 1
    for shift in (-2, -1, 1, 2):
        exists = (place + shift >= 0) & (place + shift < count)
        ready = ready + jnp.where(exists, 1, 0)

        @pl.when(exists)
        def _():
            pl.semaphore_signal(
                barrier, inc=1, device_id={"seq": place + shift}, device_id_type=MESH
            )

    for turn in range(1, head_count):
        pl.semaphore_signal(
            barrier, inc=1, device_id={"head": lax.rem(me + turn, head_count)},
            device_id_type=MESH,
        )

    def remote(src, dst, send, recv, **where):
        return pltpu.make_async_remote_copy(
            src_ref=src, dst_ref=dst, send_sem=send, recv_sem=recv, device_id=where,
            device_id_type=MESH,
        )

    def halo_up():
        return remote(x_ref.at[pl.ds(tok - edge, edge)], low, send_small.at[0],
                      recv_small.at[0], seq=place + 1)

    def halo_down():
        return remote(x_ref.at[pl.ds(0, edge)], high, send_small.at[1],
                      recv_small.at[1], seq=place - 1)

    def totals():
        return remote(tot.at[0], tot.at[1], send_small.at[2], recv_small.at[2], seq=partner)

    pl.semaphore_wait(barrier, ready)

    @pl.when(place < count - 1)
    def _():
        halo_up().start()

    @pl.when(place > 0)
    def _():
        halo_down().start()

    @pl.when(place == 0)
    def _():
        low[...] = jnp.zeros_like(low)

    @pl.when(place == count - 1)
    def _():
        high[...] = jnp.zeros_like(high)

    row_id = lax.broadcasted_iota(jnp.int32, (SPAN, SPAN), 0)
    col_id = lax.broadcasted_iota(jnp.int32, (SPAN, SPAN), 1)
    lower = row_id >= col_id
    upper = row_id <= col_id
    tri = jnp.where(upper, 1.0, 0.0).astype(BF16)
    for j in range(blocks):
        here = pl.ds(j * SPAN, SPAN)
        decay = ld_ref[:, here]
        step = step_ref[:, here]
        hi, mid, rest = split_three(decay)
        cs = mm(hi, tri) + mm(mid, tri) + mm(rest, tri)
        ecs = cs - decay
        last = cs[:, SPAN - 1 : SPAN]
        log_step = jnp.log(step)
        held[0:heads, here] = cs
        held[heads : 2 * heads, here] = ecs
        held[2 * heads : 4 * heads, here] = jnp.zeros((2 * heads, SPAN), F32)
        row_a = cs - log_step
        row_b = ecs + log_step
        for g in range(tiles):
            part = slice(g * per_tile, (g + 1) * per_tile)
            rows_ab[g, 0:per_tile, here] = row_a[part]
            rows_ab[g, per_tile : 2 * per_tile, here] = row_b[part]
    cols[...] = held[...].T
    own_total = cols[SPAN - 1 : SPAN, :]
    for j in range(1, blocks):
        own_total = own_total + cols[(j + 1) * SPAN - 1 : (j + 1) * SPAN, :]
    tot[0] = jnp.broadcast_to(own_total, tot.shape[1:])
    for j in range(blocks):
        here = pl.ds(j * SPAN, SPAN)
        cs = held[0:heads, here]
        ecs = held[heads : 2 * heads, here]
        step = step_ref[:, here]
        last = cs[:, SPAN - 1 : SPAN]
        held[0:heads, here] = jnp.exp(last - cs) * step
        held[heads : 2 * heads, here] = jnp.exp(ecs) * step
        held[2 * heads : 3 * heads, here] = jnp.exp(cs)
        held[3 * heads : 4 * heads, here] = jnp.exp(last - ecs)
        gram[j] = lax.dot_general(
            c_ref[here, :], b_ref[here, :], (((1,), (1,)), ((), ())), preferred_element_type=F32
        )
    totals().start()
    full = held[...].T
    hi = full.astype(BF16)
    quant[:, 0 : 4 * heads] = hi
    quant[:, 4 * heads : 8 * heads] = (full - hi.astype(F32)).astype(BF16)
    acc[...] = jnp.zeros_like(acc)

    @pl.when(place > 0)
    def _():
        halo_down().wait_send()
        halo_up().wait_recv()

    @pl.when(place < count - 1)
    def _():
        halo_up().wait_send()
        halo_down().wait_recv()

    totals().wait()
    scales = jnp.concatenate([jnp.exp(tot[0, 0:1, :]), jnp.exp(tot[1, 0:1, :]), skip_ref[...],
                              jnp.zeros((5, 4 * heads), F32)], axis=0)
    head = lax.broadcasted_iota(jnp.int32, (4 * heads, TILE), 0)
    lane_head = lax.broadcasted_iota(jnp.int32, (4 * heads, TILE), 1) // head_dim
    hi, mid, rest = split_three(scales)
    for i in range(tiles):
        spread = jnp.where(lane_head + i * per_tile == head, 1.0, 0.0).astype(BF16)
        wide[i] = mm(hi, spread) + mm(mid, spread) + mm(rest, spread)

    def lanes_of(i):
        return pl.ds(pl.multiple_of(i * TILE, TILE), TILE)

    def conv_tile(i):
        lanes = lanes_of(i)
        pad[pl.ds(8, tok), :] = x_ref[:, lanes].astype(F32)
        pad[pl.ds(0, 8), :] = low[pl.ds(edge - 8, 8), lanes].astype(F32)
        pad[pl.ds(8 + tok, 8), :] = high[pl.ds(0, 8), lanes].astype(F32)
        sel = [selector(i, q, heads, head_dim) for q in range(4)]
        ends = []
        for j in range(blocks):
            first = j * SPAN
            fwd = jnp.zeros((SPAN, TILE), F32)
            rev = jnp.zeros((SPAN, TILE), F32)
            for k in range(KCONV):
                w = w_ref[k : k + 1, lanes]
                fwd = fwd + w * pad[pl.ds(8 - reach + k + first, SPAN), :]
                rev = rev + w * pad[pl.ds(8 + reach - k + first, SPAN), :]
            here = pl.ds(first, SPAN)
            fwd = silu(fwd).astype(BF16)
            rev = silu(rev).astype(BF16)
            fwd_all[i, here, :] = fwd
            rev_all[i, here, :] = rev
            rates = quant[here, :]
            to_f = (fwd.astype(F32) * mm(rates, sel[0])).astype(BF16)
            to_r = (rev.astype(F32) * mm(rates, sel[1])).astype(BF16)
            b_rows = b_ref[here, :]
            turned = (((0,), (0,)), ((), ()))
            ends.append((
                lax.dot_general(b_rows, to_f, turned, preferred_element_type=F32),
                lax.dot_general(b_rows, to_r, turned, preferred_element_type=F32),
            ))
        last = mm(quant[pl.ds(tok - 16, 16), :], sel[2])[15:16, :]
        first = mm(quant[pl.ds(0, 16), :], sel[3])[0:1, :]
        (f0, r0), (f1, r1) = ends
        end_all[0, i] = (last * f0 + f1).astype(BF16)
        end_all[1, i] = (first * r1 + r0).astype(BF16)
        loc_f[i] = f0.astype(BF16)
        loc_r[i] = r1.astype(BF16)

    def chain_copy(strand, i, to):
        return remote(out_chain.at[strand, i], got_chain.at[strand, i],
                      send_chain.at[strand, i], recv_chain.at[strand, i], seq=to)

    def swap_copy(strand, i):
        return remote(out_swap.at[strand, i], got_swap.at[strand, i],
                      send_swap.at[strand, i], recv_swap.at[strand, i], seq=partner)

    strands = (
        (0, line, side, place + 2, place - 2),
        (1, lines - 1 - line, 1 - side, place - 2, place + 2),
    )

    def carry_turn(s):
        for strand, depth, second, after, before in strands:
            i = s - LAG * depth

            @pl.when((i >= 0) & (i < tiles))
            def _():
                early = jnp.where(second == 0, 1.0, 0.0)
                own = wide[i][0:1, :]
                other = wide[i][1:2, :]
                end = end_all[strand, i].astype(F32)

                @pl.when(depth > 0)
                def _():
                    chain_copy(strand, i, before).wait_recv()

                @pl.when(depth == 0)
                def _():
                    got_chain[strand, i] = jnp.zeros(got_chain.shape[2:], BF16)

                came = got_chain[strand, i].astype(F32)
                with_own = early * (own * came + end) + (1.0 - early) * came
                out_swap[strand, i] = with_own.astype(BF16)

                @pl.when(depth < lines - 1)
                def _():
                    grown = early * other + (1.0 - early)
                    out_chain[strand, i] = (own * other * came + grown * end).astype(BF16)
                    chain_copy(strand, i, after).start()

                swap_copy(strand, i).start()

    def inner_tile(i):
        turned = pltpu.roll(cols[...], 4 * heads - i * per_tile, 1)
        lane = lax.broadcasted_iota(jnp.int32, (SPAN, 128), 1) // head_dim
        for j in range(blocks):
            here = pl.ds(j * SPAN, SPAN)
            mat = gram[j]
            for p in range(TILE // 128):
                lanes = slice(p * 128, (p + 1) * 128)
                fwd = fwd_all[i, here, lanes]
                rev = rev_all[i, here, lanes]
                total = None
                for q in range(pair):
                    h = p * pair + q
                    cs = turned[j * SPAN : (j + 1) * SPAN, h : h + 1]
                    ecs = turned[j * SPAN : (j + 1) * SPAN, heads + h : heads + h + 1]
                    row_a = rows_ab[i, h : h + 1, here]
                    row_b = rows_ab[i, per_tile + h : per_tile + h + 1, here]
                    weights = mat * jnp.exp(jnp.where(lower, cs - row_a, row_b - ecs))
                    below = jnp.where(lower, weights, 0.0).astype(BF16)
                    above = jnp.where(upper, weights, 0.0).astype(BF16)
                    got = mm(below, fwd) + mm(above, rev)
                    total = got if total is None else jnp.where(lane >= q, got, total)
                skip = wide[i, 2:3, lanes]
                total_all[i, here, lanes] = total + skip * (fwd.astype(F32) + rev.astype(F32))

    def last_tile(i):
        lanes = lanes_of(i)
        arrived = []
        for strand, depth, second, after, before in strands:
            early = jnp.where(second == 0, 1.0, 0.0)
            other = wide[i][1:2, :]
            swap_copy(strand, i).wait()
            came = got_chain[strand, i].astype(F32)
            kept = (early + (1.0 - early) * other) * came
            arrived.append(kept + got_swap[strand, i].astype(F32))

            @pl.when(depth < lines - 1)
            def _():
                chain_copy(strand, i, after).wait_send()

        in_f, in_r = arrived
        sel_f = selector(i, 2, heads, head_dim)
        sel_r = selector(i, 3, heads, head_dim)
        wide_f = [mm(quant[pl.ds(j * SPAN, SPAN), :], sel_f) for j in range(2)]
        wide_r = [mm(quant[pl.ds(j * SPAN, SPAN), :], sel_r) for j in range(2)]
        next_f = loc_f[i].astype(F32) + wide_f[0][SPAN - 1 : SPAN, :] * in_f
        next_r = loc_r[i].astype(F32) + wide_r[1][0:1, :] * in_r
        start_f = (in_f.astype(BF16), next_f.astype(BF16))
        start_r = (next_r.astype(BF16), in_r.astype(BF16))
        for j in range(blocks):
            here = pl.ds(j * SPAN, SPAN)
            c_rows = c_ref[here, :]
            total = total_all[i, here, :] + wide_f[j] * mm(c_rows, start_f[j])
            total = total + wide_r[j] * mm(c_rows, start_r[j])
            gated = total * silu(z_ref[here, lanes].astype(F32))
            total_all[i, here, :] = gated
            square = gated * gated
            for p in range(TILE // 128):
                acc[here, :] += square[:, p * 128 : (p + 1) * 128]

    def conv_turn(s, _):
        conv_tile(s)
        carry_turn(s)
        return 0

    def inner_turn(s, _):
        inner_tile(s - tiles)
        carry_turn(s)
        return 0

    def drain_turn(s, _):
        carry_turn(s)
        return 0

    def last_turn(i, _):
        last_tile(i)
        return 0

    turns = tiles + LAG * (lines - 1)
    lax.fori_loop(0, tiles, conv_turn, 0)
    lax.fori_loop(tiles, 2 * tiles, inner_turn, 0)
    if turns > 2 * tiles:
        lax.fori_loop(2 * tiles, turns, drain_turn, 0)
    lax.fori_loop(0, tiles, last_turn, 0)

    sums[...] = lax.dot_general(
        jnp.ones((8, 128), F32), acc[...], (((1,), (1,)), ((), ())),
        preferred_element_type=F32, precision=HIGH,
    )

    def sum_copy(turn):
        return remote(sums, sums_got.at[turn - 1], send_sum.at[turn - 1], recv_sum.at[turn - 1],
                      head=lax.rem(me + turn, head_count))

    for turn in range(1, head_count):
        sum_copy(turn).start()
    for turn in range(1, head_count):
        sum_copy(turn).wait()
    square = sums[...]
    for turn in range(1, head_count):
        square = square + sums_got[turn - 1]
    pick = jnp.where(lax.broadcasted_iota(jnp.int32, (8, TILE), 0) == 0, 1.0, 0.0)
    square = lax.dot_general(
        square, pick, (((0,), (0,)), ((), ())), preferred_element_type=F32, precision=HIGH
    )
    acc2 = lax.rsqrt(square / (head_count * chan) + EPS)
    pad[pl.ds(0, tok), :] = acc2

    def scale_turn(i, _):
        lanes = lanes_of(i)
        out_ref[:, lanes] = (total_all[i] * pad[pl.ds(0, tok), :] * gain_ref[:, lanes]).astype(
            BF16
        )
        return 0

    lax.fori_loop(0, tiles, scale_turn, 0)


def on_device(count, head_count, x_in, z_gate, b_proj, c_proj, step_size, log_decay, conv_weight,
              skip_gain, norm_gain):
    tok, chan = x_in.shape
    heads = step_size.shape[1]
    head_dim = chan // heads
    state = b_proj.shape[1]
    tiles = chan // TILE
    per_tile = TILE // head_dim
    edge = 16
    skip = jnp.pad(skip_gain[None, :], ((0, 0), (0, 3 * heads)))
    slots = pltpu.VMEM((2, tiles, state, TILE), BF16)
    local = pltpu.VMEM((tiles, state, TILE), BF16)
    sems = pltpu.SemaphoreType.DMA((2, tiles))
    others = max(head_count - 1, 1)
    whole = pl.BlockSpec(memory_space=pltpu.VMEM)
    return pl.pallas_call(
        functools.partial(mixer_kernel, count, head_count),
        out_shape=jax.ShapeDtypeStruct((tok, chan), BF16),
        in_specs=[whole] * 9,
        out_specs=whole,
        scratch_shapes=[
            pltpu.VMEM((edge, chan), BF16),
            pltpu.VMEM((edge, chan), BF16),
            pltpu.VMEM((2, 8, 4 * heads), F32),
            pltpu.VMEM((tiles, 8, TILE), F32),
            pltpu.VMEM((4 * heads, tok), F32),
            pltpu.VMEM((tok, 8 * heads), BF16),
            pltpu.VMEM((tok, 4 * heads), F32),
            pltpu.VMEM((tiles, 2 * per_tile, tok), F32),
            pltpu.VMEM((tok // SPAN, SPAN, SPAN), F32),
            pltpu.VMEM((tok + 16, TILE), F32),
            pltpu.VMEM((tiles, tok, TILE), BF16),
            pltpu.VMEM((tiles, tok, TILE), BF16),
            pltpu.VMEM((tiles, tok, TILE), F32),
            slots, local, local, slots, slots, slots, slots,
            pltpu.VMEM((tok, 128), F32),
            pltpu.VMEM((8, tok), F32),
            pltpu.VMEM((others, 8, tok), F32),
            sems, sems, sems, sems,
            pltpu.SemaphoreType.DMA((3,)),
            pltpu.SemaphoreType.DMA((3,)),
            pltpu.SemaphoreType.DMA((others,)),
            pltpu.SemaphoreType.DMA((others,)),
        ],
        compiler_params=pltpu.CompilerParams(
            collective_id=0, has_side_effects=True, vmem_limit_bytes=60 << 20
        ),
        name="mixer",
    )(x_in, z_gate, b_proj, c_proj, step_size.T, log_decay.T, conv_weight, skip,
      norm_gain[None, :])


def solution(mesh):
    return jax.shard_map(
        functools.partial(on_device, mesh.shape["seq"], mesh.shape["head"]),
        mesh=mesh,
        in_specs=(
            P(("grp", "seq"), "head"),
            P(("grp", "seq"), "head"),
            P(("grp", "seq"), None),
            P(("grp", "seq"), None),
            P(("grp", "seq"), "head"),
            P(("grp", "seq"), "head"),
            P(None, "head"),
            P("head"),
            P("head"),
        ),
        out_specs=P(("grp", "seq"), "head"),
        check_vma=False,
    )
```

```python
import functools

import jax
import jax.numpy as jnp
from jax import lax
from jax.experimental import pallas as pl
from jax.experimental.pallas import tpu as pltpu
from jax.sharding import PartitionSpec as P

SPAN = 256
KCONV = 4
EPS = 1e-05
TILE = 256
MESH = pl.DeviceIdType.MESH
F32 = jnp.float32
BF16 = jnp.bfloat16


def mm(a, b):
    return jnp.dot(a, b, preferred_element_type=F32)


def split_three(a):
    hi = a.astype(BF16)
    rest = a - hi.astype(F32)
    mid = rest.astype(BF16)
    low = (rest - mid.astype(F32)).astype(BF16)
    return hi, mid, low


def silu(v):
    half = 0.5 * v
    return half + half * jnp.tanh(half)


LAG = 3
ROWS = 64
HALF = SPAN // 2


def mixer_kernel(count, head_count, x_hbm, z_hbm, b_ref, c_ref, step_ref, ld_ref, w_ref, skip_ref,
                 gain_ref, out_ref, x_ref, z_ref, base, ready_f, ready_r, low, high, tot, wide, held, quant, cols, rows_ab, gram, pad,
                 fwd_all, rev_all, total_all, end_all, loc_f, loc_r, out_chain, out_swap,
                 got_chain, got_swap, acc, sums, sums_got, send_chain, send_swap, recv_chain,
                 recv_swap, send_small, recv_small, send_sum, recv_sum, load_sem):
    tok, chan = out_ref.shape
    heads = step_ref.shape[0]
    head_dim = chan // heads
    state = b_ref.shape[1]
    tiles = chan // TILE
    per_tile = TILE // head_dim
    pair = 128 // head_dim
    blocks = tok // SPAN
    reach = KCONV - 1
    edge = low.shape[0]
    place = lax.axis_index("seq")
    lines = count // 2
    line = place // 2
    side = place - 2 * line
    partner = place + 1 - 2 * side
    me = lax.axis_index("head")

    load_x = pltpu.make_async_copy(x_hbm, x_ref, load_sem.at[0])
    load_z = pltpu.make_async_copy(z_hbm, z_ref, load_sem.at[1])
    load_x.start()
    load_z.start()
    barrier = pltpu.get_barrier_semaphore()
    ready = head_count - 1
    for shift in (-2, -1, 1, 2):
        exists = (place + shift >= 0) & (place + shift < count)
        ready = ready + jnp.where(exists, 1, 0)

        @pl.when(exists)
        def _():
            pl.semaphore_signal(
                barrier, inc=1, device_id={"seq": place + shift}, device_id_type=MESH
            )

    for turn in range(1, head_count):
        pl.semaphore_signal(
            barrier, inc=1, device_id={"head": lax.rem(me + turn, head_count)},
            device_id_type=MESH,
        )

    def remote(src, dst, send, recv, **where):
        return pltpu.make_async_remote_copy(
            src_ref=src, dst_ref=dst, send_sem=send, recv_sem=recv, device_id=where,
            device_id_type=MESH,
        )

    def halo_up():
        return remote(x_hbm.at[pl.ds(tok - edge, edge)], low, send_small.at[0],
                      recv_small.at[0], seq=place + 1)

    def halo_down():
        return remote(x_hbm.at[pl.ds(0, edge)], high, send_small.at[1],
                      recv_small.at[1], seq=place - 1)

    def totals():
        return remote(tot.at[0], tot.at[1], send_small.at[2], recv_small.at[2], seq=partner)

    pl.semaphore_wait(barrier, ready)

    @pl.when(place < count - 1)
    def _():
        halo_up().start()

    @pl.when(place > 0)
    def _():
        halo_down().start()

    @pl.when(place == 0)
    def _():
        low[...] = jnp.zeros_like(low)

    @pl.when(place == count - 1)
    def _():
        high[...] = jnp.zeros_like(high)

    row_id = lax.broadcasted_iota(jnp.int32, (SPAN, SPAN), 0)
    col_id = lax.broadcasted_iota(jnp.int32, (SPAN, SPAN), 1)
    lower = row_id >= col_id
    upper = row_id <= col_id
    tri = jnp.where(upper, 1.0, 0.0).astype(BF16)
    for j in range(blocks):
        here = pl.ds(j * SPAN, SPAN)
        decay = ld_ref[:, here]
        step = step_ref[:, here]
        hi, mid, rest = split_three(decay)
        cs = mm(hi, tri) + mm(mid, tri) + mm(rest, tri)
        ecs = cs - decay
        last = cs[:, SPAN - 1 : SPAN]
        log_step = jnp.log(step)
        held[0:heads, here] = cs
        held[heads : 2 * heads, here] = ecs
        held[2 * heads : 4 * heads, here] = jnp.zeros((2 * heads, SPAN), F32)
        row_a = cs - log_step
        row_b = ecs + log_step
        for g in range(tiles):
            part = slice(g * per_tile, (g + 1) * per_tile)
            rows_ab[g, 0:per_tile, here] = row_a[part]
            rows_ab[g, per_tile : 2 * per_tile, here] = row_b[part]
    cols[...] = held[...].T
    own_total = cols[SPAN - 1 : SPAN, :]
    for j in range(1, blocks):
        own_total = own_total + cols[(j + 1) * SPAN - 1 : (j + 1) * SPAN, :]
    tot[0] = jnp.broadcast_to(own_total, tot.shape[1:])
    quantities = []
    for j in range(blocks):
        here = pl.ds(j * SPAN, SPAN)
        cs = held[0:heads, here]
        ecs = held[heads : 2 * heads, here]
        step = step_ref[:, here]
        last = cs[:, SPAN - 1 : SPAN]
        parts = (jnp.exp(last - cs) * step, jnp.exp(ecs) * step, jnp.exp(cs), jnp.exp(last - ecs))
        quantities.append(parts)
        gram[j] = lax.dot_general(
            c_ref[here, :], b_ref[here, :], (((1,), (1,)), ((), ())), preferred_element_type=F32
        )
    totals().start()
    group = 4 * per_tile
    for j in range(blocks):
        here = pl.ds(j * SPAN, SPAN)
        for q in range(4):
            for g in range(tiles):
                first = g * group + q * per_tile
                held[first : first + per_tile, here] = quantities[j][q][
                    g * per_tile : (g + 1) * per_tile
                ]
    base[...] = jnp.zeros_like(base)
    row = lax.broadcasted_iota(jnp.int32, (group, 4 * TILE), 0)
    lane = lax.broadcasted_iota(jnp.int32, (group, 4 * TILE), 1)
    base[(tiles - 1) * group : tiles * group, :] = jnp.where(
        row == lane // head_dim, 1.0, 0.0
    ).astype(BF16)
    tot[2] = jnp.zeros(tot.shape[1:], F32)
    tot[2, 0:1, 0:heads] = skip_ref[...]
    full = held[...].T
    hi = full.astype(BF16)
    quant[:, 0 : 4 * heads] = hi
    quant[:, 4 * heads : 8 * heads] = (full - hi.astype(F32)).astype(BF16)
    acc[...] = jnp.zeros_like(acc)

    @pl.when(place > 0)
    def _():
        halo_down().wait_send()
        halo_up().wait_recv()

    @pl.when(place < count - 1)
    def _():
        halo_up().wait_send()
        halo_down().wait_recv()

    totals().wait()
    scales = jnp.concatenate([jnp.exp(tot[0, 0:1, :]), jnp.exp(tot[1, 0:1, :]), tot[2, 0:1, :],
                              jnp.zeros((5, 4 * heads), F32)], axis=0)
    head = lax.broadcasted_iota(jnp.int32, (4 * heads, TILE), 0)
    lane_head = lax.broadcasted_iota(jnp.int32, (4 * heads, TILE), 1) // head_dim
    hi, mid, rest = split_three(scales)
    for i in range(tiles):
        spread = jnp.where(lane_head + i * per_tile == head, 1.0, 0.0).astype(BF16)
        wide[i] = mm(hi, spread) + mm(mid, spread) + mm(rest, spread)

    def selector(i, q):
        rows = pl.ds(pl.multiple_of((tiles - 1 - i) * group, 16), 4 * heads)
        part = base[rows, q * TILE : (q + 1) * TILE]
        return jnp.concatenate([part, part], axis=0)

    def lanes_of(i):
        return pl.ds(pl.multiple_of(i * TILE, TILE), TILE)

    def conv_tile(i):
        for p in range(TILE // 128):
            lanes = pl.ds(pl.multiple_of(i * TILE + p * 128, 128), 128)
            pad[p, pl.ds(8, tok), :] = x_ref[:, lanes].astype(F32)
            pad[p, pl.ds(0, 8), :] = low[pl.ds(edge - 8, 8), lanes].astype(F32)
            pad[p, pl.ds(8 + tok, 8), :] = high[pl.ds(0, 8), lanes].astype(F32)
        ends = []
        for j in range(blocks):
            here = pl.ds(j * SPAN, SPAN)
            rates = quant[here, :]
            rate_f = mm(rates, selector(i, 0))
            rate_r = mm(rates, selector(i, 1))
            for p in range(TILE // 128):
                part = slice(p * 128, (p + 1) * 128)
                taps = [
                    w_ref[k : k + 1, pl.ds(pl.multiple_of(i * TILE + p * 128, 128), 128)]
                    for k in range(KCONV)
                ]
                for r in range(0, SPAN, ROWS):
                    first = j * SPAN + r
                    fwd = taps[0] * pad[p, pl.ds(8 - reach + first, ROWS), :]
                    rev = taps[0] * pad[p, pl.ds(8 + reach + first, ROWS), :]
                    for k in range(1, KCONV):
                        fwd = fwd + taps[k] * pad[p, pl.ds(8 - reach + k + first, ROWS), :]
                        rev = rev + taps[k] * pad[p, pl.ds(8 + reach - k + first, ROWS), :]
                    fwd = silu(fwd).astype(BF16)
                    rev = silu(rev).astype(BF16)
                    rows = pl.ds(first, ROWS)
                    fwd_all[i, rows, part] = fwd
                    rev_all[i, rows, part] = rev
                    ready_f[rows, part] = (
                        fwd.astype(F32) * rate_f[r : r + ROWS, part]
                    ).astype(BF16)
                    ready_r[rows, part] = (
                        rev.astype(F32) * rate_r[r : r + ROWS, part]
                    ).astype(BF16)
            b_rows = b_ref[here, :]
            turned = (((0,), (0,)), ((), ()))
            ends.append((
                lax.dot_general(b_rows, ready_f[here, :], turned, preferred_element_type=F32),
                lax.dot_general(b_rows, ready_r[here, :], turned, preferred_element_type=F32),
            ))
        last = mm(quant[pl.ds(tok - 16, 16), :], selector(i, 2))[15:16, :]
        first = mm(quant[pl.ds(0, 16), :], selector(i, 3))[0:1, :]
        (f0, r0), (f1, r1) = ends
        end_all[0, i] = (last * f0 + f1).astype(BF16)
        end_all[1, i] = (first * r1 + r0).astype(BF16)
        loc_f[i] = f0.astype(BF16)
        loc_r[i] = r1.astype(BF16)

    def chain_copy(strand, i, to):
        return remote(out_chain.at[strand, i], got_chain.at[strand, i],
                      send_chain.at[strand, i], recv_chain.at[strand, i], seq=to)

    def swap_copy(strand, i):
        return remote(out_swap.at[strand, i], got_swap.at[strand, i],
                      send_swap.at[strand, i], recv_swap.at[strand, i], seq=partner)

    strands = (
        (0, line, side, place + 2, place - 2),
        (1, lines - 1 - line, 1 - side, place - 2, place + 2),
    )

    def carry_turn(s):
        for strand, depth, second, after, before in strands:
            i = s - LAG * depth

            @pl.when((i >= 0) & (i < tiles))
            def _():
                early = jnp.where(second == 0, 1.0, 0.0)
                own = wide[i][0:1, :]
                other = wide[i][1:2, :]
                end = end_all[strand, i].astype(F32)

                @pl.when(depth > 0)
                def _():
                    chain_copy(strand, i, before).wait_recv()

                @pl.when(depth == 0)
                def _():
                    got_chain[strand, i] = jnp.zeros(got_chain.shape[2:], BF16)

                came = got_chain[strand, i].astype(F32)
                with_own = early * (own * came + end) + (1.0 - early) * came
                out_swap[strand, i] = with_own.astype(BF16)

                @pl.when(depth < lines - 1)
                def _():
                    grown = early * other + (1.0 - early)
                    out_chain[strand, i] = (own * other * came + grown * end).astype(BF16)
                    chain_copy(strand, i, after).start()

                swap_copy(strand, i).start()

    def inner_tile(i):
        turned = pltpu.roll(cols[...], 4 * heads - i * per_tile, 1)
        lane = lax.broadcasted_iota(jnp.int32, (SPAN, 128), 1) // head_dim
        row_half = lax.broadcasted_iota(jnp.int32, (HALF, HALF), 0)
        col_half = lax.broadcasted_iota(jnp.int32, (HALF, HALF), 1)
        lower_half = row_half >= col_half
        upper_half = row_half <= col_half
        for j in range(blocks):
            here = pl.ds(j * SPAN, SPAN)
            for p in range(TILE // 128):
                lanes = slice(p * 128, (p + 1) * 128)
                fwd = fwd_all[i, here, lanes]
                rev = rev_all[i, here, lanes]
                below, above = [], []
                for q in range(pair):
                    h = p * pair + q
                    ats = [slice(u * HALF, (u + 1) * HALF) for u in range(2)]
                    cs = [turned[j * SPAN + u * HALF : j * SPAN + (u + 1) * HALF, h : h + 1]
                          for u in range(2)]
                    ecs = [turned[j * SPAN + u * HALF : j * SPAN + (u + 1) * HALF,
                                  heads + h : heads + h + 1] for u in range(2)]
                    cells = [pl.ds(j * SPAN + u * HALF, HALF) for u in range(2)]
                    row_a = [rows_ab[i, h : h + 1, cells[u]] for u in range(2)]
                    row_b = [rows_ab[i, per_tile + h : per_tile + h + 1, cells[u]]
                             for u in range(2)]
                    lows, ups = [], []
                    for u in range(2):
                        weights = gram[j, ats[u], ats[u]] * jnp.exp(
                            jnp.where(lower_half, cs[u] - row_a[u], row_b[u] - ecs[u])
                        )
                        lows.append(jnp.where(lower_half, weights, 0.0).astype(BF16))
                        ups.append(jnp.where(upper_half, weights, 0.0).astype(BF16))
                    left = (gram[j, ats[1], ats[0]] * jnp.exp(cs[1] - row_a[0])).astype(BF16)
                    right = (gram[j, ats[0], ats[1]] * jnp.exp(row_b[1] - ecs[0])).astype(BF16)
                    none = jnp.zeros((HALF, HALF), BF16)
                    below.append(jnp.concatenate([lows[0], none], axis=1))
                    below.append(jnp.concatenate([left, lows[1]], axis=1))
                    above.append(jnp.concatenate([ups[0], right], axis=1))
                    above.append(jnp.concatenate([none, ups[1]], axis=1))
                got = mm(jnp.concatenate(below, axis=0), fwd)
                got = got + mm(jnp.concatenate(above, axis=0), rev)
                total = got[0:SPAN]
                for q in range(1, pair):
                    total = jnp.where(lane >= q, got[q * SPAN : (q + 1) * SPAN], total)
                skip = wide[i, 2:3, lanes]
                total_all[i, here, lanes] = total + skip * (fwd.astype(F32) + rev.astype(F32))

    def last_tile(i):
        lanes = lanes_of(i)
        arrived = []
        for strand, depth, second, after, before in strands:
            early = jnp.where(second == 0, 1.0, 0.0)
            other = wide[i][1:2, :]
            swap_copy(strand, i).wait()
            came = got_chain[strand, i].astype(F32)
            kept = (early + (1.0 - early) * other) * came
            arrived.append(kept + got_swap[strand, i].astype(F32))

            @pl.when(depth < lines - 1)
            def _():
                chain_copy(strand, i, after).wait_send()

        in_f, in_r = arrived
        sel_f = selector(i, 2)
        sel_r = selector(i, 3)
        wide_f = [mm(quant[pl.ds(j * SPAN, SPAN), :], sel_f) for j in range(2)]
        wide_r = [mm(quant[pl.ds(j * SPAN, SPAN), :], sel_r) for j in range(2)]
        next_f = loc_f[i].astype(F32) + wide_f[0][SPAN - 1 : SPAN, :] * in_f
        next_r = loc_r[i].astype(F32) + wide_r[1][0:1, :] * in_r
        start_f = (in_f.astype(BF16), next_f.astype(BF16))
        start_r = (next_r.astype(BF16), in_r.astype(BF16))
        for j in range(blocks):
            here = pl.ds(j * SPAN, SPAN)
            c_rows = c_ref[here, :]
            total = total_all[i, here, :] + wide_f[j] * mm(c_rows, start_f[j])
            total = total + wide_r[j] * mm(c_rows, start_r[j])
            gated = total * silu(z_ref[here, lanes].astype(F32))
            total_all[i, here, :] = gated
            square = gated * gated
            for p in range(TILE // 128):
                acc[here, :] += square[:, p * 128 : (p + 1) * 128]

    def conv_turn(s, _):
        conv_tile(s)
        carry_turn(s)
        return 0

    def inner_turn(s, _):
        inner_tile(s - tiles)
        carry_turn(s)
        return 0

    def drain_turn(s, _):
        carry_turn(s)
        return 0

    def last_turn(i, _):
        last_tile(i)
        return 0

    load_x.wait()
    turns = tiles + LAG * (lines - 1)
    lax.fori_loop(0, tiles, conv_turn, 0)
    lax.fori_loop(tiles, 2 * tiles, inner_turn, 0)
    if turns > 2 * tiles:
        lax.fori_loop(2 * tiles, turns, drain_turn, 0)
    load_z.wait()
    lax.fori_loop(0, tiles, last_turn, 0)

    sums[...] = jnp.broadcast_to(jnp.sum(acc[...].T, axis=0, keepdims=True), sums.shape)

    def sum_copy(turn):
        return remote(sums, sums_got.at[turn - 1], send_sum.at[turn - 1], recv_sum.at[turn - 1],
                      head=lax.rem(me + turn, head_count))

    for turn in range(1, head_count):
        sum_copy(turn).start()
    for turn in range(1, head_count):
        sum_copy(turn).wait()
    square = sums[...]
    for turn in range(1, head_count):
        square = square + sums_got[turn - 1]
    scale = lax.rsqrt(square[0:1, :] / (head_count * chan) + EPS)
    acc[...] = jnp.broadcast_to(scale, (128, tok)).T

    def scale_turn(i, _):
        for p in range(TILE // 128):
            lanes = pl.ds(pl.multiple_of(i * TILE + p * 128, 128), 128)
            out_ref[:, lanes] = (
                total_all[i, :, p * 128 : (p + 1) * 128] * acc[...] * gain_ref[:, lanes]
            ).astype(BF16)
        return 0

    lax.fori_loop(0, tiles, scale_turn, 0)


def on_device(count, head_count, x_in, z_gate, b_proj, c_proj, step_size, log_decay, conv_weight,
              skip_gain, norm_gain):
    tok, chan = x_in.shape
    heads = step_size.shape[1]
    head_dim = chan // heads
    state = b_proj.shape[1]
    tiles = chan // TILE
    per_tile = TILE // head_dim
    edge = 16
    slots = pltpu.VMEM((2, tiles, state, TILE), BF16)
    local = pltpu.VMEM((tiles, state, TILE), BF16)
    sems = pltpu.SemaphoreType.DMA((2, tiles))
    others = max(head_count - 1, 1)
    whole = pl.BlockSpec(memory_space=pltpu.VMEM)
    return pl.pallas_call(
        functools.partial(mixer_kernel, count, head_count),
        out_shape=jax.ShapeDtypeStruct((tok, chan), BF16),
        in_specs=[pl.BlockSpec(memory_space=pl.ANY)] * 2 + [whole] * 7,
        out_specs=whole,
        scratch_shapes=[
            pltpu.VMEM((tok, chan), BF16),
            pltpu.VMEM((tok, chan), BF16),
            pltpu.VMEM(((2 * tiles - 1) * 4 * per_tile, 4 * TILE), BF16),
            pltpu.VMEM((tok, TILE), BF16),
            pltpu.VMEM((tok, TILE), BF16),
            pltpu.VMEM((edge, chan), BF16),
            pltpu.VMEM((edge, chan), BF16),
            pltpu.VMEM((3, 8, 4 * heads), F32),
            pltpu.VMEM((tiles, 8, TILE), F32),
            pltpu.VMEM((4 * heads, tok), F32),
            pltpu.VMEM((tok, 8 * heads), BF16),
            pltpu.VMEM((tok, 4 * heads), F32),
            pltpu.VMEM((tiles, 2 * per_tile, tok), F32),
            pltpu.VMEM((tok // SPAN, SPAN, SPAN), F32),
            pltpu.VMEM((TILE // 128, tok + 16, 128), F32),
            pltpu.VMEM((tiles, tok, TILE), BF16),
            pltpu.VMEM((tiles, tok, TILE), BF16),
            pltpu.VMEM((tiles, tok, TILE), F32),
            slots, local, local, slots, slots, slots, slots,
            pltpu.VMEM((tok, 128), F32),
            pltpu.VMEM((8, tok), F32),
            pltpu.VMEM((others, 8, tok), F32),
            sems, sems, sems, sems,
            pltpu.SemaphoreType.DMA((3,)),
            pltpu.SemaphoreType.DMA((3,)),
            pltpu.SemaphoreType.DMA((others,)),
            pltpu.SemaphoreType.DMA((others,)),
            pltpu.SemaphoreType.DMA((2,)),
        ],
        compiler_params=pltpu.CompilerParams(
            collective_id=0, has_side_effects=True, vmem_limit_bytes=60 << 20
        ),
        name="mixer",
    )(x_in, z_gate, b_proj, c_proj, step_size.T, log_decay.T, conv_weight,
      skip_gain[None, :],      norm_gain[None, :])


def solution(mesh):
    return jax.shard_map(
        functools.partial(on_device, mesh.shape["seq"], mesh.shape["head"]),
        mesh=mesh,
        in_specs=(
            P(("grp", "seq"), "head"),
            P(("grp", "seq"), "head"),
            P(("grp", "seq"), None),
            P(("grp", "seq"), None),
            P(("grp", "seq"), "head"),
            P(("grp", "seq"), "head"),
            P(None, "head"),
            P("head"),
            P("head"),
        ),
        out_specs=P(("grp", "seq"), "head"),
        check_vma=False,
    )
```

```python
import functools

import jax
import jax.numpy as jnp
from jax import lax
from jax.experimental import pallas as pl
from jax.experimental.pallas import tpu as pltpu
from jax.sharding import PartitionSpec as P

SPAN = 256
KCONV = 4
EPS = 1e-05
TILE = 256
MESH = pl.DeviceIdType.MESH
F32 = jnp.float32
BF16 = jnp.bfloat16


def mm(a, b):
    return jnp.dot(a, b, preferred_element_type=F32)


def split_three(a):
    hi = a.astype(BF16)
    rest = a - hi.astype(F32)
    mid = rest.astype(BF16)
    low = (rest - mid.astype(F32)).astype(BF16)
    return hi, mid, low


def silu(v):
    half = 0.5 * v
    return half + half * jnp.tanh(half)


LAG = 2
SWAP_LAG = 2
ROWS = 64
HALF = SPAN // 2


def mixer_kernel(count, head_count, x_hbm, z_hbm, b_ref, c_ref, step_ref, ld_ref, w_ref, skip_ref,
                 out_hbm, scale_ref, x_ref, z_ref, base, ready_f, ready_r, low, high, tot, wide, held, quant, cols, rows_ab, gram, pad,
                 fwd_all, rev_all, total_all, end_all, loc_f, loc_r, out_chain, got_chain,
                 got_swap, got_back, acc, sums, sums_got, send_chain, send_swap, send_back, recv_chain,
                 recv_swap, recv_back, send_small, recv_small, send_sum, recv_sum, load_sem,
                 store_sem):
    tok, chan = x_ref.shape
    heads = step_ref.shape[0]
    head_dim = chan // heads
    state = b_ref.shape[1]
    tiles = chan // TILE
    per_tile = TILE // head_dim
    pair = 128 // head_dim
    blocks = tok // SPAN
    reach = KCONV - 1
    edge = low.shape[0]
    place = lax.axis_index("seq")
    lines = count // 2
    line = place // 2
    side = place - 2 * line
    partner = place + 1 - 2 * side
    me = lax.axis_index("head")

    load_x = pltpu.make_async_copy(x_hbm, x_ref, load_sem.at[0])
    load_z = pltpu.make_async_copy(z_hbm, z_ref, load_sem.at[1])
    load_x.start()
    load_z.start()
    barrier = pltpu.get_barrier_semaphore()
    ready = head_count - 1
    for shift in (-2, -1, 1, 2):
        exists = (place + shift >= 0) & (place + shift < count)
        ready = ready + jnp.where(exists, 1, 0)

        @pl.when(exists)
        def _():
            pl.semaphore_signal(
                barrier, inc=1, device_id={"seq": place + shift}, device_id_type=MESH
            )

    for turn in range(1, head_count):
        pl.semaphore_signal(
            barrier, inc=1, device_id={"head": lax.rem(me + turn, head_count)},
            device_id_type=MESH,
        )

    def remote(src, dst, send, recv, **where):
        return pltpu.make_async_remote_copy(
            src_ref=src, dst_ref=dst, send_sem=send, recv_sem=recv, device_id=where,
            device_id_type=MESH,
        )

    def halo_up():
        return remote(x_hbm.at[pl.ds(tok - edge, edge)], low, send_small.at[0],
                      recv_small.at[0], seq=place + 1)

    def halo_down():
        return remote(x_hbm.at[pl.ds(0, edge)], high, send_small.at[1],
                      recv_small.at[1], seq=place - 1)

    def totals():
        return remote(tot.at[0], tot.at[1], send_small.at[2], recv_small.at[2], seq=partner)

    pl.semaphore_wait(barrier, ready)

    @pl.when(place < count - 1)
    def _():
        halo_up().start()

    @pl.when(place > 0)
    def _():
        halo_down().start()

    @pl.when(place == 0)
    def _():
        low[...] = jnp.zeros_like(low)

    @pl.when(place == count - 1)
    def _():
        high[...] = jnp.zeros_like(high)

    row_id = lax.broadcasted_iota(jnp.int32, (SPAN, SPAN), 0)
    col_id = lax.broadcasted_iota(jnp.int32, (SPAN, SPAN), 1)
    lower = row_id >= col_id
    upper = row_id <= col_id
    tri = jnp.where(upper, 1.0, 0.0).astype(BF16)
    for j in range(blocks):
        here = pl.ds(j * SPAN, SPAN)
        decay = ld_ref[:, here]
        step = step_ref[:, here]
        hi, mid, rest = split_three(decay)
        cs = mm(hi, tri) + mm(mid, tri) + mm(rest, tri)
        ecs = cs - decay
        last = cs[:, SPAN - 1 : SPAN]
        log_step = jnp.log(step)
        held[0:heads, here] = cs
        held[heads : 2 * heads, here] = ecs
        held[2 * heads : 4 * heads, here] = jnp.zeros((2 * heads, SPAN), F32)
        row_a = cs - log_step
        row_b = ecs + log_step
        for g in range(tiles):
            part = slice(g * per_tile, (g + 1) * per_tile)
            rows_ab[g, 0:per_tile, here] = row_a[part]
            rows_ab[g, per_tile : 2 * per_tile, here] = row_b[part]
    cols[...] = held[...].T
    own_total = cols[SPAN - 1 : SPAN, :]
    for j in range(1, blocks):
        own_total = own_total + cols[(j + 1) * SPAN - 1 : (j + 1) * SPAN, :]
    tot[0] = jnp.broadcast_to(own_total, tot.shape[1:])
    quantities = []
    for j in range(blocks):
        here = pl.ds(j * SPAN, SPAN)
        cs = held[0:heads, here]
        ecs = held[heads : 2 * heads, here]
        step = step_ref[:, here]
        last = cs[:, SPAN - 1 : SPAN]
        parts = (jnp.exp(last - cs) * step, jnp.exp(ecs) * step, jnp.exp(cs), jnp.exp(last - ecs))
        quantities.append(parts)
        gram[j] = lax.dot_general(
            c_ref[here, :], b_ref[here, :], (((1,), (1,)), ((), ())), preferred_element_type=F32
        )
    totals().start()
    group = 4 * per_tile
    for j in range(blocks):
        here = pl.ds(j * SPAN, SPAN)
        for q in range(4):
            for g in range(tiles):
                first = g * group + q * per_tile
                held[first : first + per_tile, here] = quantities[j][q][
                    g * per_tile : (g + 1) * per_tile
                ]
    base[...] = jnp.zeros_like(base)
    row = lax.broadcasted_iota(jnp.int32, (group, 4 * TILE), 0)
    lane = lax.broadcasted_iota(jnp.int32, (group, 4 * TILE), 1)
    base[(tiles - 1) * group : tiles * group, :] = jnp.where(
        row == lane // head_dim, 1.0, 0.0
    ).astype(BF16)
    tot[2] = jnp.zeros(tot.shape[1:], F32)
    tot[2, 0:1, 0:heads] = skip_ref[...]
    full = held[...].T
    hi = full.astype(BF16)
    quant[:, 0 : 4 * heads] = hi
    quant[:, 4 * heads : 8 * heads] = (full - hi.astype(F32)).astype(BF16)
    acc[...] = jnp.zeros_like(acc)

    @pl.when(place > 0)
    def _():
        halo_down().wait_send()
        halo_up().wait_recv()

    @pl.when(place < count - 1)
    def _():
        halo_up().wait_send()
        halo_down().wait_recv()

    totals().wait()
    scales = jnp.concatenate([jnp.exp(tot[0, 0:1, :]), jnp.exp(tot[1, 0:1, :]), tot[2, 0:1, :],
                              jnp.zeros((5, 4 * heads), F32)], axis=0)
    head = lax.broadcasted_iota(jnp.int32, (4 * heads, TILE), 0)
    lane_head = lax.broadcasted_iota(jnp.int32, (4 * heads, TILE), 1) // head_dim
    hi, mid, rest = split_three(scales)
    for i in range(tiles):
        spread = jnp.where(lane_head + i * per_tile == head, 1.0, 0.0).astype(BF16)
        wide[i] = mm(hi, spread) + mm(mid, spread) + mm(rest, spread)

    def selector(i, q):
        rows = pl.ds(pl.multiple_of((tiles - 1 - i) * group, 16), 4 * heads)
        part = base[rows, q * TILE : (q + 1) * TILE]
        return jnp.concatenate([part, part], axis=0)

    def lanes_of(i):
        return pl.ds(pl.multiple_of(i * TILE, TILE), TILE)

    def conv_tile(i):
        for p in range(TILE // 128):
            lanes = pl.ds(pl.multiple_of(i * TILE + p * 128, 128), 128)
            pad[p, pl.ds(8, tok), :] = x_ref[:, lanes].astype(F32)
            pad[p, pl.ds(0, 8), :] = low[pl.ds(edge - 8, 8), lanes].astype(F32)
            pad[p, pl.ds(8 + tok, 8), :] = high[pl.ds(0, 8), lanes].astype(F32)
        ends = []
        for j in range(blocks):
            here = pl.ds(j * SPAN, SPAN)
            rates = quant[here, :]
            rate_f = mm(rates, selector(i, 0))
            rate_r = mm(rates, selector(i, 1))
            for p in range(TILE // 128):
                part = slice(p * 128, (p + 1) * 128)
                taps = [
                    w_ref[k : k + 1, pl.ds(pl.multiple_of(i * TILE + p * 128, 128), 128)]
                    for k in range(KCONV)
                ]
                for r in range(0, SPAN, ROWS):
                    first = j * SPAN + r
                    fwd = taps[0] * pad[p, pl.ds(8 - reach + first, ROWS), :]
                    rev = taps[0] * pad[p, pl.ds(8 + reach + first, ROWS), :]
                    for k in range(1, KCONV):
                        fwd = fwd + taps[k] * pad[p, pl.ds(8 - reach + k + first, ROWS), :]
                        rev = rev + taps[k] * pad[p, pl.ds(8 + reach - k + first, ROWS), :]
                    fwd = silu(fwd).astype(BF16)
                    rev = silu(rev).astype(BF16)
                    rows = pl.ds(first, ROWS)
                    fwd_all[i, rows, part] = fwd
                    rev_all[i, rows, part] = rev
                    ready_f[rows, part] = (
                        fwd.astype(F32) * rate_f[r : r + ROWS, part]
                    ).astype(BF16)
                    ready_r[rows, part] = (
                        rev.astype(F32) * rate_r[r : r + ROWS, part]
                    ).astype(BF16)
            b_rows = b_ref[here, :]
            turned = (((0,), (0,)), ((), ()))
            ends.append((
                lax.dot_general(b_rows, ready_f[here, :], turned, preferred_element_type=F32),
                lax.dot_general(b_rows, ready_r[here, :], turned, preferred_element_type=F32),
            ))
        last = mm(quant[pl.ds(tok - 16, 16), :], selector(i, 2))[15:16, :]
        first = mm(quant[pl.ds(0, 16), :], selector(i, 3))[0:1, :]
        (f0, r0), (f1, r1) = ends
        end_all[0, i] = (last * f0 + f1).astype(BF16)
        end_all[1, i] = (first * r1 + r0).astype(BF16)
        loc_f[i] = f0.astype(BF16)
        loc_r[i] = r1.astype(BF16)

    lead = side
    follow = 1 - side
    follow_depth = jnp.where(side == 1, line, lines - 1 - line)
    lead_depth = jnp.where(side == 0, line, lines - 1 - line)
    after = place + 4 * side - 2

    def lead_copy(i):
        return remote(end_all.at[lead, i], got_swap.at[i], send_swap.at[i], recv_swap.at[i],
                      seq=partner)

    def chain_copy(i):
        return remote(out_chain.at[i], got_chain.at[i], send_chain.at[i], recv_chain.at[i],
                      seq=after)

    def back_copy(i):
        return remote(got_chain.at[i], got_back.at[i], send_back.at[i], recv_back.at[i],
                      seq=partner)

    def carry_turn(s):
        i = s - SWAP_LAG - LAG * follow_depth

        @pl.when((i >= 0) & (i < tiles))
        def _():
            @pl.when(follow_depth > 0)
            def _():
                chain_copy(i).wait_recv()
                back_copy(i).start()

            @pl.when(follow_depth == 0)
            def _():
                got_chain[i] = jnp.zeros(got_chain.shape[1:], BF16)

            lead_copy(i).wait_recv()

            @pl.when(follow_depth < lines - 1)
            def _():
                own = wide[i][0:1, :]
                other = wide[i][1:2, :]
                grown = own * (other * got_chain[i].astype(F32) + got_swap[i].astype(F32))
                out_chain[i] = (grown + end_all[follow, i].astype(F32)).astype(BF16)
                chain_copy(i).start()

    def inner_tile(i):
        turned = pltpu.roll(cols[...], 4 * heads - i * per_tile, 1)
        lane = lax.broadcasted_iota(jnp.int32, (SPAN, 128), 1) // head_dim
        row_half = lax.broadcasted_iota(jnp.int32, (HALF, HALF), 0)
        col_half = lax.broadcasted_iota(jnp.int32, (HALF, HALF), 1)
        lower_half = row_half >= col_half
        upper_half = row_half <= col_half
        for j in range(blocks):
            here = pl.ds(j * SPAN, SPAN)
            for p in range(TILE // 128):
                lanes = slice(p * 128, (p + 1) * 128)
                fwd = fwd_all[i, here, lanes]
                rev = rev_all[i, here, lanes]
                below, above = [], []
                for q in range(pair):
                    h = p * pair + q
                    ats = [slice(u * HALF, (u + 1) * HALF) for u in range(2)]
                    cs = [turned[j * SPAN + u * HALF : j * SPAN + (u + 1) * HALF, h : h + 1]
                          for u in range(2)]
                    ecs = [turned[j * SPAN + u * HALF : j * SPAN + (u + 1) * HALF,
                                  heads + h : heads + h + 1] for u in range(2)]
                    cells = [pl.ds(j * SPAN + u * HALF, HALF) for u in range(2)]
                    row_a = [rows_ab[i, h : h + 1, cells[u]] for u in range(2)]
                    row_b = [rows_ab[i, per_tile + h : per_tile + h + 1, cells[u]]
                             for u in range(2)]
                    lows, ups = [], []
                    for u in range(2):
                        weights = gram[j, ats[u], ats[u]] * jnp.exp(
                            jnp.where(lower_half, cs[u] - row_a[u], row_b[u] - ecs[u])
                        )
                        lows.append(jnp.where(lower_half, weights, 0.0).astype(BF16))
                        ups.append(jnp.where(upper_half, weights, 0.0).astype(BF16))
                    left = (gram[j, ats[1], ats[0]] * jnp.exp(cs[1] - row_a[0])).astype(BF16)
                    right = (gram[j, ats[0], ats[1]] * jnp.exp(row_b[1] - ecs[0])).astype(BF16)
                    none = jnp.zeros((HALF, HALF), BF16)
                    below.append(jnp.concatenate([lows[0], none], axis=1))
                    below.append(jnp.concatenate([left, lows[1]], axis=1))
                    above.append(jnp.concatenate([ups[0], right], axis=1))
                    above.append(jnp.concatenate([none, ups[1]], axis=1))
                got = mm(jnp.concatenate(below, axis=0), fwd)
                got = got + mm(jnp.concatenate(above, axis=0), rev)
                total = got[0:SPAN]
                for q in range(1, pair):
                    total = jnp.where(lane >= q, got[q * SPAN : (q + 1) * SPAN], total)
                skip = wide[i, 2:3, lanes]
                total_all[i, here, lanes] = total + skip * (fwd.astype(F32) + rev.astype(F32))

    def last_tile(i):
        lanes = lanes_of(i)

        @pl.when(lead_depth > 0)
        def _():
            back_copy(i).wait_recv()

        @pl.when(lead_depth == 0)
        def _():
            got_back[i] = jnp.zeros(got_back.shape[1:], BF16)

        @pl.when(follow_depth > 0)
        def _():
            back_copy(i).wait_send()

        @pl.when(follow_depth < lines - 1)
        def _():
            chain_copy(i).wait_send()

        lead_copy(i).wait_send()
        came = wide[i][1:2, :] * got_chain[i].astype(F32) + got_swap[i].astype(F32)
        led = got_back[i].astype(F32)
        in_f = jnp.where(side == 0, led, came)
        in_r = jnp.where(side == 0, came, led)
        sel_f = selector(i, 2)
        sel_r = selector(i, 3)
        wide_f = [mm(quant[pl.ds(j * SPAN, SPAN), :], sel_f) for j in range(2)]
        wide_r = [mm(quant[pl.ds(j * SPAN, SPAN), :], sel_r) for j in range(2)]
        next_f = loc_f[i].astype(F32) + wide_f[0][SPAN - 1 : SPAN, :] * in_f
        next_r = loc_r[i].astype(F32) + wide_r[1][0:1, :] * in_r
        start_f = (in_f.astype(BF16), next_f.astype(BF16))
        start_r = (next_r.astype(BF16), in_r.astype(BF16))
        for j in range(blocks):
            here = pl.ds(j * SPAN, SPAN)
            c_rows = c_ref[here, :]
            total = total_all[i, here, :] + wide_f[j] * mm(c_rows, start_f[j])
            total = total + wide_r[j] * mm(c_rows, start_r[j])
            gated = total * silu(z_ref[here, lanes].astype(F32))
            z_ref[here, lanes] = gated.astype(BF16)
            square = gated * gated
            for p in range(TILE // 128):
                acc[here, :] += square[:, p * 128 : (p + 1) * 128]

    def conv_turn(s, _):
        conv_tile(s)
        lead_copy(s).start()
        carry_turn(s)
        return 0

    def inner_turn(s, _):
        inner_tile(s - tiles)
        carry_turn(s)
        return 0

    def drain_turn(s, _):
        carry_turn(s)
        return 0

    def store(i):
        lanes = lanes_of(i)
        return pltpu.make_async_copy(z_ref.at[:, lanes], out_hbm.at[:, lanes], store_sem.at[i])

    def last_turn(i, _):
        last_tile(i)
        store(i).start()
        return 0

    load_x.wait()
    turns = tiles + SWAP_LAG + LAG * (lines - 1)
    lax.fori_loop(0, tiles, conv_turn, 0)
    lax.fori_loop(tiles, 2 * tiles, inner_turn, 0)
    if turns > 2 * tiles:
        lax.fori_loop(2 * tiles, turns, drain_turn, 0)
    load_z.wait()
    lax.fori_loop(0, tiles, last_turn, 0)

    sums[...] = jnp.broadcast_to(jnp.sum(acc[...].T, axis=0, keepdims=True), sums.shape)

    def sum_copy(turn):
        return remote(sums, sums_got.at[turn - 1], send_sum.at[turn - 1], recv_sum.at[turn - 1],
                      head=lax.rem(me + turn, head_count))

    for turn in range(1, head_count):
        sum_copy(turn).start()
    for turn in range(1, head_count):
        sum_copy(turn).wait()
    square = sums[...]
    for turn in range(1, head_count):
        square = square + sums_got[turn - 1]
    scale = lax.rsqrt(square[0:1, :] / (head_count * chan) + EPS)
    scale_ref[...] = jnp.broadcast_to(scale, (128, tok)).T

    def store_turn(i, _):
        store(i).wait()
        return 0

    lax.fori_loop(0, tiles, store_turn, 0)


def scale_kernel(gated_ref, scale_ref, gain_ref, out_ref):
    scale = scale_ref[...]
    for p in range(out_ref.shape[1] // 128):
        lanes = slice(p * 128, (p + 1) * 128)
        out_ref[:, lanes] = (
            gated_ref[:, lanes].astype(F32) * scale * gain_ref[:, lanes]
        ).astype(BF16)


def on_device(count, head_count, x_in, z_gate, b_proj, c_proj, step_size, log_decay, conv_weight,
              skip_gain, norm_gain):
    tok, chan = x_in.shape
    heads = step_size.shape[1]
    head_dim = chan // heads
    state = b_proj.shape[1]
    tiles = chan // TILE
    per_tile = TILE // head_dim
    edge = 16
    slots = pltpu.VMEM((2, tiles, state, TILE), BF16)
    local = pltpu.VMEM((tiles, state, TILE), BF16)
    sems = pltpu.SemaphoreType.DMA((tiles,))
    others = max(head_count - 1, 1)
    whole = pl.BlockSpec(memory_space=pltpu.VMEM)
    gated, scale = pl.pallas_call(
        functools.partial(mixer_kernel, count, head_count),
        out_shape=(
            jax.ShapeDtypeStruct((tok, chan), BF16),
            jax.ShapeDtypeStruct((tok, 128), F32),
        ),
        in_specs=[pl.BlockSpec(memory_space=pl.ANY)] * 2 + [whole] * 6,
        out_specs=(pl.BlockSpec(memory_space=pl.ANY), whole),
        scratch_shapes=[
            pltpu.VMEM((tok, chan), BF16),
            pltpu.VMEM((tok, chan), BF16),
            pltpu.VMEM(((2 * tiles - 1) * 4 * per_tile, 4 * TILE), BF16),
            pltpu.VMEM((tok, TILE), BF16),
            pltpu.VMEM((tok, TILE), BF16),
            pltpu.VMEM((edge, chan), BF16),
            pltpu.VMEM((edge, chan), BF16),
            pltpu.VMEM((3, 8, 4 * heads), F32),
            pltpu.VMEM((tiles, 8, TILE), F32),
            pltpu.VMEM((4 * heads, tok), F32),
            pltpu.VMEM((tok, 8 * heads), BF16),
            pltpu.VMEM((tok, 4 * heads), F32),
            pltpu.VMEM((tiles, 2 * per_tile, tok), F32),
            pltpu.VMEM((tok // SPAN, SPAN, SPAN), F32),
            pltpu.VMEM((TILE // 128, tok + 16, 128), F32),
            pltpu.VMEM((tiles, tok, TILE), BF16),
            pltpu.VMEM((tiles, tok, TILE), BF16),
            pltpu.VMEM((tiles, tok, TILE), F32),
            slots, local, local, local, local, local, local,
            pltpu.VMEM((tok, 128), F32),
            pltpu.VMEM((8, tok), F32),
            pltpu.VMEM((others, 8, tok), F32),
            sems, sems, sems, sems, sems, sems,
            pltpu.SemaphoreType.DMA((3,)),
            pltpu.SemaphoreType.DMA((3,)),
            pltpu.SemaphoreType.DMA((others,)),
            pltpu.SemaphoreType.DMA((others,)),
            pltpu.SemaphoreType.DMA((2,)),
            sems,
        ],
        compiler_params=pltpu.CompilerParams(
            collective_id=0, has_side_effects=True, vmem_limit_bytes=60 << 20
        ),
        name="mixer",
    )(x_in, z_gate, b_proj, c_proj, step_size.T, log_decay.T, conv_weight,
      skip_gain[None, :])
    part = tok // 4
    tall = pl.BlockSpec((part, chan), lambda i: (i, 0))
    return pl.pallas_call(
        scale_kernel,
        grid=(tok // part,),
        out_shape=jax.ShapeDtypeStruct((tok, chan), BF16),
        in_specs=[tall, pl.BlockSpec((part, 128), lambda i: (i, 0)),
                  pl.BlockSpec((1, chan), lambda i: (0, 0))],
        out_specs=tall,
        name="scale",
    )(gated, scale, norm_gain[None, :])


def solution(mesh):
    return jax.shard_map(
        functools.partial(on_device, mesh.shape["seq"], mesh.shape["head"]),
        mesh=mesh,
        in_specs=(
            P(("grp", "seq"), "head"),
            P(("grp", "seq"), "head"),
            P(("grp", "seq"), None),
            P(("grp", "seq"), None),
            P(("grp", "seq"), "head"),
            P(("grp", "seq"), "head"),
            P(None, "head"),
            P("head"),
            P("head"),
        ),
        out_specs=P(("grp", "seq"), "head"),
        check_vma=False,
    )
```

```python
import functools

import jax
import jax.numpy as jnp
from jax import lax
from jax.experimental import pallas as pl
from jax.experimental.pallas import tpu as pltpu
from jax.sharding import PartitionSpec as P

SPAN = 256
KCONV = 4
EPS = 1e-05
TILE = 256
MESH = pl.DeviceIdType.MESH
F32 = jnp.float32
BF16 = jnp.bfloat16


def mm(a, b):
    return jnp.dot(a, b, preferred_element_type=F32)


def split_three(a):
    hi = a.astype(BF16)
    rest = a - hi.astype(F32)
    mid = rest.astype(BF16)
    low = (rest - mid.astype(F32)).astype(BF16)
    return hi, mid, low


def silu(v):
    half = 0.5 * v
    return half + half * jnp.tanh(half)


LAG = 2
ROWS = 64
HALF = SPAN // 2


def mixer_kernel(count, head_count, x_hbm, z_hbm, b_ref, c_ref, step_ref, ld_ref, w_ref, skip_ref,
                 gain_ref, out_ref, x_ref, z_ref, base, ready_f, ready_r, low, high, tot, wide, held, quant, cols, rows_ab, gram, pad,
                 fwd_all, rev_all, total_all, end_all, loc_f, loc_r, out_chain, out_swap,
                 got_chain, got_swap, acc, sums, sums_got, send_chain, send_swap, recv_chain,
                 recv_swap, send_small, recv_small, send_sum, recv_sum, load_sem):
    tok, chan = out_ref.shape
    heads = step_ref.shape[0]
    head_dim = chan // heads
    state = b_ref.shape[1]
    tiles = chan // TILE
    per_tile = TILE // head_dim
    pair = 128 // head_dim
    blocks = tok // SPAN
    reach = KCONV - 1
    edge = low.shape[0]
    place = lax.axis_index("seq")
    lines = count // 2
    line = place // 2
    side = place - 2 * line
    partner = place + 1 - 2 * side
    me = lax.axis_index("head")

    load_x = pltpu.make_async_copy(x_hbm, x_ref, load_sem.at[0])
    load_z = pltpu.make_async_copy(z_hbm, z_ref, load_sem.at[1])
    load_x.start()
    load_z.start()
    barrier = pltpu.get_barrier_semaphore()
    ready = head_count - 1
    for shift in (-2, -1, 1, 2):
        exists = (place + shift >= 0) & (place + shift < count)
        ready = ready + jnp.where(exists, 1, 0)

        @pl.when(exists)
        def _():
            pl.semaphore_signal(
                barrier, inc=1, device_id={"seq": place + shift}, device_id_type=MESH
            )

    for turn in range(1, head_count):
        pl.semaphore_signal(
            barrier, inc=1, device_id={"head": lax.rem(me + turn, head_count)},
            device_id_type=MESH,
        )

    def remote(src, dst, send, recv, **where):
        return pltpu.make_async_remote_copy(
            src_ref=src, dst_ref=dst, send_sem=send, recv_sem=recv, device_id=where,
            device_id_type=MESH,
        )

    def halo_up():
        return remote(x_hbm.at[pl.ds(tok - edge, edge)], low, send_small.at[0],
                      recv_small.at[0], seq=place + 1)

    def halo_down():
        return remote(x_hbm.at[pl.ds(0, edge)], high, send_small.at[1],
                      recv_small.at[1], seq=place - 1)

    def totals():
        return remote(tot.at[0], tot.at[1], send_small.at[2], recv_small.at[2], seq=partner)

    pl.semaphore_wait(barrier, ready)

    @pl.when(place < count - 1)
    def _():
        halo_up().start()

    @pl.when(place > 0)
    def _():
        halo_down().start()

    @pl.when(place == 0)
    def _():
        low[...] = jnp.zeros_like(low)

    @pl.when(place == count - 1)
    def _():
        high[...] = jnp.zeros_like(high)

    row_id = lax.broadcasted_iota(jnp.int32, (SPAN, SPAN), 0)
    col_id = lax.broadcasted_iota(jnp.int32, (SPAN, SPAN), 1)
    lower = row_id >= col_id
    upper = row_id <= col_id
    tri = jnp.where(upper, 1.0, 0.0).astype(BF16)
    for j in range(blocks):
        here = pl.ds(j * SPAN, SPAN)
        decay = ld_ref[:, here]
        step = step_ref[:, here]
        hi, mid, rest = split_three(decay)
        cs = mm(hi, tri) + mm(mid, tri) + mm(rest, tri)
        ecs = cs - decay
        last = cs[:, SPAN - 1 : SPAN]
        log_step = jnp.log(step)
        held[0:heads, here] = cs
        held[heads : 2 * heads, here] = ecs
        held[2 * heads : 4 * heads, here] = jnp.zeros((2 * heads, SPAN), F32)
        row_a = cs - log_step
        row_b = ecs + log_step
        for g in range(tiles):
            part = slice(g * per_tile, (g + 1) * per_tile)
            rows_ab[g, 0:per_tile, here] = row_a[part]
            rows_ab[g, per_tile : 2 * per_tile, here] = row_b[part]
    cols[...] = held[...].T
    own_total = cols[SPAN - 1 : SPAN, :]
    for j in range(1, blocks):
        own_total = own_total + cols[(j + 1) * SPAN - 1 : (j + 1) * SPAN, :]
    tot[0] = jnp.broadcast_to(own_total, tot.shape[1:])
    quantities = []
    for j in range(blocks):
        here = pl.ds(j * SPAN, SPAN)
        cs = held[0:heads, here]
        ecs = held[heads : 2 * heads, here]
        step = step_ref[:, here]
        last = cs[:, SPAN - 1 : SPAN]
        parts = (jnp.exp(last - cs) * step, jnp.exp(ecs) * step, jnp.exp(cs), jnp.exp(last - ecs))
        quantities.append(parts)
        gram[j] = lax.dot_general(
            c_ref[here, :], b_ref[here, :], (((1,), (1,)), ((), ())), preferred_element_type=F32
        )
    totals().start()
    group = 4 * per_tile
    for j in range(blocks):
        here = pl.ds(j * SPAN, SPAN)
        for q in range(4):
            for g in range(tiles):
                first = g * group + q * per_tile
                held[first : first + per_tile, here] = quantities[j][q][
                    g * per_tile : (g + 1) * per_tile
                ]
    base[...] = jnp.zeros_like(base)
    row = lax.broadcasted_iota(jnp.int32, (group, 4 * TILE), 0)
    lane = lax.broadcasted_iota(jnp.int32, (group, 4 * TILE), 1)
    base[(tiles - 1) * group : tiles * group, :] = jnp.where(
        row == lane // head_dim, 1.0, 0.0
    ).astype(BF16)
    tot[2] = jnp.zeros(tot.shape[1:], F32)
    tot[2, 0:1, 0:heads] = skip_ref[...]
    full = held[...].T
    hi = full.astype(BF16)
    quant[:, 0 : 4 * heads] = hi
    quant[:, 4 * heads : 8 * heads] = (full - hi.astype(F32)).astype(BF16)
    acc[...] = jnp.zeros_like(acc)

    @pl.when(place > 0)
    def _():
        halo_down().wait_send()
        halo_up().wait_recv()

    @pl.when(place < count - 1)
    def _():
        halo_up().wait_send()
        halo_down().wait_recv()

    totals().wait()
    scales = jnp.concatenate([jnp.exp(tot[0, 0:1, :]), jnp.exp(tot[1, 0:1, :]), tot[2, 0:1, :],
                              jnp.zeros((5, 4 * heads), F32)], axis=0)
    head = lax.broadcasted_iota(jnp.int32, (4 * heads, TILE), 0)
    lane_head = lax.broadcasted_iota(jnp.int32, (4 * heads, TILE), 1) // head_dim
    hi, mid, rest = split_three(scales)
    for i in range(tiles):
        spread = jnp.where(lane_head + i * per_tile == head, 1.0, 0.0).astype(BF16)
        wide[i] = mm(hi, spread) + mm(mid, spread) + mm(rest, spread)

    def selector(i, q):
        rows = pl.ds(pl.multiple_of((tiles - 1 - i) * group, 16), 4 * heads)
        part = base[rows, q * TILE : (q + 1) * TILE]
        return jnp.concatenate([part, part], axis=0)

    def lanes_of(i):
        return pl.ds(pl.multiple_of(i * TILE, TILE), TILE)

    def conv_tile(i):
        for p in range(TILE // 128):
            lanes = pl.ds(pl.multiple_of(i * TILE + p * 128, 128), 128)
            pad[p, pl.ds(8, tok), :] = x_ref[:, lanes].astype(F32)
            pad[p, pl.ds(0, 8), :] = low[pl.ds(edge - 8, 8), lanes].astype(F32)
            pad[p, pl.ds(8 + tok, 8), :] = high[pl.ds(0, 8), lanes].astype(F32)
        ends = []
        for j in range(blocks):
            here = pl.ds(j * SPAN, SPAN)
            rates = quant[here, :]
            rate_f = mm(rates, selector(i, 0))
            rate_r = mm(rates, selector(i, 1))
            for p in range(TILE // 128):
                part = slice(p * 128, (p + 1) * 128)
                taps = [
                    w_ref[k : k + 1, pl.ds(pl.multiple_of(i * TILE + p * 128, 128), 128)]
                    for k in range(KCONV)
                ]
                for r in range(0, SPAN, ROWS):
                    first = j * SPAN + r
                    fwd = taps[0] * pad[p, pl.ds(8 - reach + first, ROWS), :]
                    rev = taps[0] * pad[p, pl.ds(8 + reach + first, ROWS), :]
                    for k in range(1, KCONV):
                        fwd = fwd + taps[k] * pad[p, pl.ds(8 - reach + k + first, ROWS), :]
                        rev = rev + taps[k] * pad[p, pl.ds(8 + reach - k + first, ROWS), :]
                    fwd = silu(fwd).astype(BF16)
                    rev = silu(rev).astype(BF16)
                    rows = pl.ds(first, ROWS)
                    fwd_all[i, rows, part] = fwd
                    rev_all[i, rows, part] = rev
                    ready_f[rows, part] = (
                        fwd.astype(F32) * rate_f[r : r + ROWS, part]
                    ).astype(BF16)
                    ready_r[rows, part] = (
                        rev.astype(F32) * rate_r[r : r + ROWS, part]
                    ).astype(BF16)
            b_rows = b_ref[here, :]
            turned = (((0,), (0,)), ((), ()))
            ends.append((
                lax.dot_general(b_rows, ready_f[here, :], turned, preferred_element_type=F32),
                lax.dot_general(b_rows, ready_r[here, :], turned, preferred_element_type=F32),
            ))
        last = mm(quant[pl.ds(tok - 16, 16), :], selector(i, 2))[15:16, :]
        first = mm(quant[pl.ds(0, 16), :], selector(i, 3))[0:1, :]
        (f0, r0), (f1, r1) = ends
        end_all[0, i] = (last * f0 + f1).astype(BF16)
        end_all[1, i] = (first * r1 + r0).astype(BF16)
        loc_f[i] = f0.astype(BF16)
        loc_r[i] = r1.astype(BF16)

    def chain_copy(strand, i, to):
        return remote(out_chain.at[strand, i], got_chain.at[strand, i],
                      send_chain.at[strand, i], recv_chain.at[strand, i], seq=to)

    def swap_copy(strand, i):
        return remote(out_swap.at[strand, i], got_swap.at[strand, i],
                      send_swap.at[strand, i], recv_swap.at[strand, i], seq=partner)

    strands = (
        (0, line, side, place + 2, place - 2),
        (1, lines - 1 - line, 1 - side, place - 2, place + 2),
    )

    def carry_turn(s):
        for strand, depth, second, after, before in strands:
            i = s - LAG * depth

            @pl.when((i >= 0) & (i < tiles))
            def _():
                early = jnp.where(second == 0, 1.0, 0.0)
                own = wide[i][0:1, :]
                other = wide[i][1:2, :]
                end = end_all[strand, i].astype(F32)

                @pl.when(depth > 0)
                def _():
                    chain_copy(strand, i, before).wait_recv()

                @pl.when(depth == 0)
                def _():
                    got_chain[strand, i] = jnp.zeros(got_chain.shape[2:], BF16)

                came = got_chain[strand, i].astype(F32)
                with_own = early * (own * came + end) + (1.0 - early) * came
                out_swap[strand, i] = with_own.astype(BF16)

                @pl.when(depth < lines - 1)
                def _():
                    grown = early * other + (1.0 - early)
                    out_chain[strand, i] = (own * other * came + grown * end).astype(BF16)
                    chain_copy(strand, i, after).start()

                swap_copy(strand, i).start()

    def inner_tile(i):
        turned = pltpu.roll(cols[...], 4 * heads - i * per_tile, 1)
        lane = lax.broadcasted_iota(jnp.int32, (SPAN, 128), 1) // head_dim
        row_half = lax.broadcasted_iota(jnp.int32, (HALF, HALF), 0)
        col_half = lax.broadcasted_iota(jnp.int32, (HALF, HALF), 1)
        lower_half = row_half >= col_half
        upper_half = row_half <= col_half
        for j in range(blocks):
            here = pl.ds(j * SPAN, SPAN)
            for p in range(TILE // 128):
                lanes = slice(p * 128, (p + 1) * 128)
                fwd = fwd_all[i, here, lanes]
                rev = rev_all[i, here, lanes]
                below, above = [], []
                for q in range(pair):
                    h = p * pair + q
                    ats = [slice(u * HALF, (u + 1) * HALF) for u in range(2)]
                    cs = [turned[j * SPAN + u * HALF : j * SPAN + (u + 1) * HALF, h : h + 1]
                          for u in range(2)]
                    ecs = [turned[j * SPAN + u * HALF : j * SPAN + (u + 1) * HALF,
                                  heads + h : heads + h + 1] for u in range(2)]
                    cells = [pl.ds(j * SPAN + u * HALF, HALF) for u in range(2)]
                    row_a = [rows_ab[i, h : h + 1, cells[u]] for u in range(2)]
                    row_b = [rows_ab[i, per_tile + h : per_tile + h + 1, cells[u]]
                             for u in range(2)]
                    lows, ups = [], []
                    for u in range(2):
                        weights = gram[j, ats[u], ats[u]] * jnp.exp(
                            jnp.where(lower_half, cs[u] - row_a[u], row_b[u] - ecs[u])
                        )
                        lows.append(jnp.where(lower_half, weights, 0.0).astype(BF16))
                        ups.append(jnp.where(upper_half, weights, 0.0).astype(BF16))
                    left = (gram[j, ats[1], ats[0]] * jnp.exp(cs[1] - row_a[0])).astype(BF16)
                    right = (gram[j, ats[0], ats[1]] * jnp.exp(row_b[1] - ecs[0])).astype(BF16)
                    none = jnp.zeros((HALF, HALF), BF16)
                    below.append(jnp.concatenate([lows[0], none], axis=1))
                    below.append(jnp.concatenate([left, lows[1]], axis=1))
                    above.append(jnp.concatenate([ups[0], right], axis=1))
                    above.append(jnp.concatenate([none, ups[1]], axis=1))
                got = mm(jnp.concatenate(below, axis=0), fwd)
                got = got + mm(jnp.concatenate(above, axis=0), rev)
                total = got[0:SPAN]
                for q in range(1, pair):
                    total = jnp.where(lane >= q, got[q * SPAN : (q + 1) * SPAN], total)
                skip = wide[i, 2:3, lanes]
                total_all[i, here, lanes] = total + skip * (fwd.astype(F32) + rev.astype(F32))

    def last_tile(i):
        lanes = lanes_of(i)
        arrived = []
        for strand, depth, second, after, before in strands:
            early = jnp.where(second == 0, 1.0, 0.0)
            other = wide[i][1:2, :]
            swap_copy(strand, i).wait()
            came = got_chain[strand, i].astype(F32)
            kept = (early + (1.0 - early) * other) * came
            arrived.append(kept + got_swap[strand, i].astype(F32))

            @pl.when(depth < lines - 1)
            def _():
                chain_copy(strand, i, after).wait_send()

        in_f, in_r = arrived
        sel_f = selector(i, 2)
        sel_r = selector(i, 3)
        wide_f = [mm(quant[pl.ds(j * SPAN, SPAN), :], sel_f) for j in range(2)]
        wide_r = [mm(quant[pl.ds(j * SPAN, SPAN), :], sel_r) for j in range(2)]
        next_f = loc_f[i].astype(F32) + wide_f[0][SPAN - 1 : SPAN, :] * in_f
        next_r = loc_r[i].astype(F32) + wide_r[1][0:1, :] * in_r
        start_f = (in_f.astype(BF16), next_f.astype(BF16))
        start_r = (next_r.astype(BF16), in_r.astype(BF16))
        for j in range(blocks):
            here = pl.ds(j * SPAN, SPAN)
            c_rows = c_ref[here, :]
            total = total_all[i, here, :] + wide_f[j] * mm(c_rows, start_f[j])
            total = total + wide_r[j] * mm(c_rows, start_r[j])
            gated = total * silu(z_ref[here, lanes].astype(F32))
            total_all[i, here, :] = gated
            square = gated * gated
            for p in range(TILE // 128):
                acc[here, :] += square[:, p * 128 : (p + 1) * 128]

    def conv_turn(s, _):
        conv_tile(s)
        carry_turn(s)
        return 0

    def inner_turn(s, _):
        inner_tile(s - tiles)
        carry_turn(s)
        return 0

    def drain_turn(s, _):
        carry_turn(s)
        return 0

    def last_turn(i, _):
        last_tile(i)
        return 0

    load_x.wait()
    turns = tiles + LAG * (lines - 1)
    lax.fori_loop(0, tiles, conv_turn, 0)
    lax.fori_loop(tiles, 2 * tiles, inner_turn, 0)
    if turns > 2 * tiles:
        lax.fori_loop(2 * tiles, turns, drain_turn, 0)
    load_z.wait()
    lax.fori_loop(0, tiles, last_turn, 0)

    sums[...] = jnp.broadcast_to(jnp.sum(acc[...].T, axis=0, keepdims=True), sums.shape)

    def sum_copy(turn):
        return remote(sums, sums_got.at[turn - 1], send_sum.at[turn - 1], recv_sum.at[turn - 1],
                      head=lax.rem(me + turn, head_count))

    for turn in range(1, head_count):
        sum_copy(turn).start()
    for turn in range(1, head_count):
        sum_copy(turn).wait()
    square = sums[...]
    for turn in range(1, head_count):
        square = square + sums_got[turn - 1]
    scale = lax.rsqrt(square[0:1, :] / (head_count * chan) + EPS)
    acc[...] = jnp.broadcast_to(scale, (128, tok)).T

    def scale_turn(i, _):
        for p in range(TILE // 128):
            lanes = pl.ds(pl.multiple_of(i * TILE + p * 128, 128), 128)
            out_ref[:, lanes] = (
                total_all[i, :, p * 128 : (p + 1) * 128] * acc[...] * gain_ref[:, lanes]
            ).astype(BF16)
        return 0

    lax.fori_loop(0, tiles, scale_turn, 0)


def on_device(count, head_count, x_in, z_gate, b_proj, c_proj, step_size, log_decay, conv_weight,
              skip_gain, norm_gain):
    tok, chan = x_in.shape
    heads = step_size.shape[1]
    head_dim = chan // heads
    state = b_proj.shape[1]
    tiles = chan // TILE
    per_tile = TILE // head_dim
    edge = 16
    slots = pltpu.VMEM((2, tiles, state, TILE), BF16)
    local = pltpu.VMEM((tiles, state, TILE), BF16)
    sems = pltpu.SemaphoreType.DMA((2, tiles))
    others = max(head_count - 1, 1)
    whole = pl.BlockSpec(memory_space=pltpu.VMEM)
    return pl.pallas_call(
        functools.partial(mixer_kernel, count, head_count),
        out_shape=jax.ShapeDtypeStruct((tok, chan), BF16),
        in_specs=[pl.BlockSpec(memory_space=pl.ANY)] * 2 + [whole] * 7,
        out_specs=whole,
        scratch_shapes=[
            pltpu.VMEM((tok, chan), BF16),
            pltpu.VMEM((tok, chan), BF16),
            pltpu.VMEM(((2 * tiles - 1) * 4 * per_tile, 4 * TILE), BF16),
            pltpu.VMEM((tok, TILE), BF16),
            pltpu.VMEM((tok, TILE), BF16),
            pltpu.VMEM((edge, chan), BF16),
            pltpu.VMEM((edge, chan), BF16),
            pltpu.VMEM((3, 8, 4 * heads), F32),
            pltpu.VMEM((tiles, 8, TILE), F32),
            pltpu.VMEM((4 * heads, tok), F32),
            pltpu.VMEM((tok, 8 * heads), BF16),
            pltpu.VMEM((tok, 4 * heads), F32),
            pltpu.VMEM((tiles, 2 * per_tile, tok), F32),
            pltpu.VMEM((tok // SPAN, SPAN, SPAN), F32),
            pltpu.VMEM((TILE // 128, tok + 16, 128), F32),
            pltpu.VMEM((tiles, tok, TILE), BF16),
            pltpu.VMEM((tiles, tok, TILE), BF16),
            pltpu.VMEM((tiles, tok, TILE), F32),
            slots, local, local, slots, slots, slots, slots,
            pltpu.VMEM((tok, 128), F32),
            pltpu.VMEM((8, tok), F32),
            pltpu.VMEM((others, 8, tok), F32),
            sems, sems, sems, sems,
            pltpu.SemaphoreType.DMA((3,)),
            pltpu.SemaphoreType.DMA((3,)),
            pltpu.SemaphoreType.DMA((others,)),
            pltpu.SemaphoreType.DMA((others,)),
            pltpu.SemaphoreType.DMA((2,)),
        ],
        compiler_params=pltpu.CompilerParams(
            collective_id=0, has_side_effects=True, vmem_limit_bytes=60 << 20
        ),
        name="mixer",
    )(x_in, z_gate, b_proj, c_proj, step_size.T, log_decay.T, conv_weight,
      skip_gain[None, :],      norm_gain[None, :])


def solution(mesh):
    return jax.shard_map(
        functools.partial(on_device, mesh.shape["seq"], mesh.shape["head"]),
        mesh=mesh,
        in_specs=(
            P(("grp", "seq"), "head"),
            P(("grp", "seq"), "head"),
            P(("grp", "seq"), None),
            P(("grp", "seq"), None),
            P(("grp", "seq"), "head"),
            P(("grp", "seq"), "head"),
            P(None, "head"),
            P("head"),
            P("head"),
        ),
        out_specs=P(("grp", "seq"), "head"),
        check_vma=False,
    )
```
